128 devices in a mesh: facet: 16 (over x, z_hi, core), sub: 4 (over y), wa: 2 (over z_lo).
Axes of the slice: x: 4, y: 4, z: 4 (z_hi: 2, z_lo: 2; z = z_hi * 2 + z_lo), core: 2. Of those that a mesh axis runs over, the one named last changes fastest.
Arguments:
- facets: float32 [16, 512, 2, 4096], P('facet'), may hold values from -6 to 6
- correction: float32 [16, 4096], P('facet'), may hold values from 0.5 to 2
- window: float32 [128], replicated, may hold values from 0.25 to 1
- offsets: int32 [8], replicated, may hold values from 0 to 4095
- phases: float32 [4, 2048], P('wa'), may hold values from -3.140625 to 3.140625
- coverage: int32 [8, 4, 2048], P('sub', 'wa'), may hold values from 0 to 3
Outputs:
- facets_out: float32 [16, 512, 2, 4096], P('facet', ('sub', 'wa'))
The draws below stay inside these ranges and needn't reach their ends.
All inputs are finite; a program needn't handle non-finite values.
Results may differ from the reference program's by a relative error of at most 0.0001.
Values sent between devices are 32-bit elements; how exact they have to be, the bound alone decides.
No kernel may reach another device: no remote copies, remote signals or barrier semaphores. Data moves between devices by JAX's collectives and lax.ppermute only.
A program may use at most 192 MiB of HBM per device.

```python
import math
import jax
import jax.numpy as jnp

YN = 4096
CM = 128
WPLANES = 4
FACETS = 16
ROWS = 512
SUBS = 8
XM = 2048


def with_ends(drawn, own_key, least, high):
    longest = drawn.shape.index(max(drawn.shape))
    spots = []
    for shift in (0, 1):
        where = [jax.random.randint(jax.random.fold_in(own_key, axis), (), 0, length) for axis, length in enumerate(drawn.shape)]
        where[longest] = (where[longest] + shift) % drawn.shape[longest]
        spots.append(tuple(where))
    return drawn.at[spots[0]].set(least).at[spots[1]].set(high)


def shard_levels(stream_key, extent, cuts, least, largest):
    def one(dim, shards_of):
        steps = jax.random.uniform(jax.random.fold_in(jax.random.fold_in(stream_key, 6), dim), (shards_of,), jnp.float32, least / len(cuts), largest / len(cuts))
        return jnp.repeat(jnp.exp(steps), extent[dim] // shards_of).reshape((-1,) + (1,) * (len(extent) - dim - 1))

    factor_of = one(*cuts[0])
    for cut in cuts[1:]:
        factor_of = factor_of * one(*cut)
    return factor_of


def bell_draw(rng, shape, spread, reach, pieces=(), kind=jnp.bfloat16):
    values = jax.random.normal(rng, shape, jnp.float32) * spread
    if len(pieces) > 0:
        values = shard_levels(rng, shape, pieces, -0.22, 0.18) * values
    return jnp.clip(values, min=-reach, max=reach).astype(kind)


def setup_inputs(seed: int = 0) -> dict:
    seeds = jax.random.split(jax.random.key(seed), 7)
    facets = bell_draw(seeds[0], (FACETS, ROWS, 2, YN), 1.0, 6.0, ((0, 16),), jnp.float32)
    correction = jnp.clip(jnp.exp(math.log(2.0) - 1.3862944 * jax.random.uniform(seeds[1], (FACETS, YN), jnp.float32) ** shard_levels(seeds[1], (FACETS, YN), ((0, 16),), -0.2, 0.2)), 0.5, 2.0)
    window = jnp.clip(jnp.exp(jax.random.uniform(seeds[2], (CM,), jnp.float32, math.log(0.25), math.log(1.0))), 0.25, 1.0)
    offsets = with_ends(jax.random.randint(seeds[3], (SUBS,), 0, YN), jax.random.fold_in(seeds[3], 1), 0, YN - 1).astype(jnp.int32)
    phases = jnp.clip(jax.random.uniform(seeds[4], (WPLANES, XM), jnp.float32, -3.140625, 3.140625), -3.140625, 3.140625)
    coverage = with_ends(jax.random.randint(seeds[5], (SUBS, WPLANES, XM), 0, 4), jax.random.fold_in(seeds[5], 1), 0, 3).astype(jnp.int32)
    return dict(facets=facets, correction=correction, window=window, offsets=offsets, phases=phases, coverage=coverage)


def reference(facets, correction, window, offsets, phases, coverage):
    pixels = (facets[:, :, 0, :] + 1j * facets[:, :, 1, :]) * correction[:, None, :]
    spectrum = jnp.fft.fft(pixels, axis=-1, norm="ortho")
    positions = (offsets[:, None] + jnp.arange(CM, dtype=jnp.int32)[None, :]) % YN
    segments = spectrum[:, :, positions] * window
    blocks = jnp.fft.ifft(segments, axis=-1, norm="ortho")
    subgrid = jnp.transpose(blocks, (1, 2, 0, 3)).reshape(ROWS, SUBS, XM)
    adjoint = jnp.zeros_like(subgrid)
    for wplane in range(WPLANES):
        kernel = jnp.exp(1j * phases[wplane])
        grid_values = jnp.fft.fft(kernel * subgrid, axis=-1, norm="ortho")
        weighted = grid_values * coverage[:, wplane, :].astype(jnp.float32)
        adjoint = adjoint + jnp.conj(kernel) * jnp.fft.ifft(weighted, axis=-1, norm="ortho")
    adjoint = adjoint / WPLANES
    returned = jnp.transpose(adjoint.reshape(ROWS, SUBS, FACETS, CM), (2, 0, 1, 3))
    back_segments = jnp.fft.fft(returned, axis=-1, norm="ortho") * window
    accumulated = jnp.zeros((FACETS, ROWS, YN), back_segments.dtype).at[:, :, positions].add(back_segments)
    result = jnp.fft.ifft(accumulated, axis=-1, norm="ortho") * correction[:, None, :]
    return jnp.stack([jnp.real(result), jnp.imag(result)], axis=2).astype(jnp.float32)
```

```python
import math

import jax
import jax.numpy as jnp
import numpy as np
from jax import lax
from jax.experimental import pallas as pl
from jax.experimental.pallas import tpu as pltpu
from jax.sharding import PartitionSpec as P

WPLANES = 4
LANES = 128
F32 = jnp.float32
BF16 = jnp.bfloat16


def trig(rows, cols, length):
    product = np.arange(rows, dtype=np.int64)[:, None] * np.arange(cols, dtype=np.int64)[None, :]
    angle = (product % length) * (2.0 * math.pi / length)
    return np.cos(angle), np.sin(angle)


def halves(table):
    high = table.astype(np.float32).astype(BF16)
    low = (table - high.astype(np.float64)).astype(np.float32).astype(BF16)
    return jnp.asarray(high), jnp.asarray(low)


def split(x):
    high = x.astype(BF16)
    return high, (x - high.astype(F32)).astype(BF16)


def mul_const(re, im, c, s):
    tiny = 1e-12
    if abs(s) < tiny:
        return (re, im) if c > 0 else (-re, -im)
    if abs(c) < tiny:
        return (-im, re) if s > 0 else (im, -re)
    if abs(abs(c) - abs(s)) < tiny:
        u = re * c
        v = im * c
        return (u - v, u + v) if c * s > 0 else (u + v, v - u)
    return re * c - im * s, re * s + im * c


def small_fft(re, im, sign):
    n = len(re)
    if n == 1:
        return re, im
    radix = 4 if n % 4 == 0 else 2
    m = n // radix
    parts = [small_fft(re[j::radix], im[j::radix], sign) for j in range(radix)]
    out_re, out_im = [None] * n, [None] * n
    for k in range(m):
        terms = []
        for j in range(radix):
            angle = sign * 2.0 * math.pi * j * k / n
            terms.append(mul_const(parts[j][0][k], parts[j][1][k], math.cos(angle), math.sin(angle)))
        if radix == 2:
            (ar, ai), (br, bi) = terms
            out_re[k], out_im[k] = ar + br, ai + bi
            out_re[k + m], out_im[k + m] = ar - br, ai - bi
        else:
            (ar, ai), (br, bi), (cr, ci), (dr, di) = terms
            sr, si, tr, ti = ar + cr, ai + ci, ar - cr, ai - ci
            ur, ui, vr, vi = br + dr, bi + di, br - dr, bi - di
            out_re[k], out_im[k] = sr + ur, si + ui
            out_re[k + 2 * m], out_im[k + 2 * m] = sr - ur, si - ui
            if sign > 0:
                out_re[k + m], out_im[k + m] = tr - vi, ti + vr
                out_re[k + 3 * m], out_im[k + 3 * m] = tr + vi, ti - vr
            else:
                out_re[k + m], out_im[k + m] = tr + vi, ti - vr
                out_re[k + 3 * m], out_im[k + 3 * m] = tr - vi, ti + vr
    return out_re, out_im


def dot_nt(a, b):
    return lax.dot_general(a, b, (((1,), (1,)), ((), ())), preferred_element_type=F32)


def dot_nn(a, b):
    return lax.dot_general(a, b, (((1,), (0,)), ((), ())), preferred_element_type=F32)


def turned_rows(re, im, part):
    left, right = [], []
    for at in range(0, re.shape[0], part):
        a, b = re[at : at + part], im[at : at + part]
        left += [a, b]
        right += [b, -a]
    return jnp.concatenate([jnp.concatenate(left, 0), jnp.concatenate(right, 0)], 1)


def forward_kernel(
    scal, facets, corr, tw_cos, tw_sin, line_hi, line_lo, block, window, out, xr, xi, yr, yi, spec, sems
):
    rows = xr.shape[0]
    outer = yr.shape[0]
    length = outer * LANES
    half = rows // 2
    groups = rows // 8
    base = pl.multiple_of(scal[0], rows)

    def copies(g):
        at = pl.ds(g * 8, 8)
        return (
            pltpu.make_async_copy(facets.at[pl.ds(base + g * 8, 8), 0, :], xr.at[at, :], sems.at[0, g]),
            pltpu.make_async_copy(facets.at[pl.ds(base + g * 8, 8), 1, :], xi.at[at, :], sems.at[1, g]),
        )

    for g in range(groups):
        for c in copies(g):
            c.start()

    def first(g, carry):
        for c in copies(g):
            c.wait()
        at = pl.ds(pl.multiple_of(g * 8, 8), 8)
        re, im = [], []
        for a in range(outer):
            scale = corr[a : a + 1, :]
            lanes = pl.ds(a * LANES, LANES)
            re.append(xr[at, lanes] * scale)
            im.append(xi[at, lanes] * scale)
        re, im = small_fft(re, im, -1.0)
        for k in range(outer):
            c, s = tw_cos[k : k + 1, :], tw_sin[k : k + 1, :]
            yr[k, at, :] = re[k] * c + im[k] * s
            yi[k, at, :] = im[k] * c - re[k] * s
        return carry

    lax.fori_loop(0, groups, first, 0)

    def second(j, carry):
        both = [turned_rows(yr[2 * j + e], yi[2 * j + e], half) for e in range(2)]
        high, low = split(jnp.concatenate(both, 0))
        z = dot_nt(line_hi[...], high) + dot_nt(line_hi[...], low) + dot_nt(line_lo[...], high)
        for e in range(2):
            spec[pl.ds(2 * j + e, LANES, stride=outer), :] = z[:, e * LANES : (e + 1) * LANES]
        return carry

    lax.fori_loop(0, outer // 2, second, 0)
    spec[length : length + LANES, :] = spec[0:LANES, :]
    table_hi, table_lo = split(block[...] * window[...])
    for s in range(out.shape[0] // 2):
        seg = spec[pl.ds(scal[1 + s], LANES), :]
        high, low = split(seg.T)
        p = dot_nn(high, table_hi) + dot_nn(low, table_hi) + dot_nn(high, table_lo)
        for h in range(2):
            a, b = p[2 * h * half : (2 * h + 1) * half], p[(2 * h + 1) * half : (2 * h + 2) * half]
            out[2 * s + h, 0:half, :] = a[:, :LANES] - b[:, LANES:]
            out[2 * s + h, half : 2 * half, :] = a[:, LANES:] + b[:, :LANES]


def middle_kernel(x, own, other, tw_cos, tw_sin, fwd_hi, fwd_lo, bwd_hi, bwd_lo, out, kc, ks, cnt, br, bi):
    outer = x.shape[0]
    rows = x.shape[1] // 2
    groups = rows // 8
    planes = own.shape[0] // 2
    per = LANES // outer
    lane_i = lax.broadcasted_iota(jnp.int32, (LANES, LANES), 0)
    lane_n = lax.broadcasted_iota(jnp.int32, (LANES, LANES), 1)
    mask = (lane_i // outer) == (lane_n % per)
    spread = (
        lax.broadcasted_iota(jnp.int32, (outer, LANES), 1) // per
        == lax.broadcasted_iota(jnp.int32, (outer, LANES), 0)
    ).astype(F32)
    fold = (
        lax.broadcasted_iota(jnp.int32, (outer, LANES), 1) % outer
        == lax.broadcasted_iota(jnp.int32, (outer, LANES), 0)
    ).astype(F32)
    for src, at in ((own, 0), (other, planes)):
        for w in range(planes):
            wide = dot_nn(src[w].T.astype(BF16), spread.astype(BF16))
            picked = jnp.where(mask, wide, 0.0).astype(BF16)
            cnt[at + w] = dot_nn(fold.astype(BF16), picked)
            kc[at + w] = jnp.cos(src[planes + w])
            ks[at + w] = jnp.sin(src[planes + w])

    out[...] = jnp.zeros(out.shape, F32)

    def plane(w, carry):
        def first(g, c2):
            top = pl.ds(pl.multiple_of(g * 8, 8), 8)
            bot = pl.ds(pl.multiple_of(rows + g * 8, 8), 8)
            re, im = [], []
            for a in range(outer):
                c, s = kc[w, a : a + 1, :], ks[w, a : a + 1, :]
                p, q = x[a, top, :], x[a, bot, :]
                re.append(p * c - q * s)
                im.append(p * s + q * c)
            re, im = small_fft(re, im, -1.0)
            for k in range(outer):
                c, s = tw_cos[k : k + 1, :], tw_sin[k : k + 1, :]
                br[k, top, :] = re[k] * c + im[k] * s
                bi[k, top, :] = im[k] * c - re[k] * s
            return c2

        lax.fori_loop(0, groups, first, 0)
        step = LANES // rows
        for k in range(0, outer, step):
            left = jnp.concatenate([br[k + e] for e in range(step)], 0)
            right = jnp.concatenate([bi[k + e] for e in range(step)], 0)
            high, low = split(jnp.concatenate([left, right], 1))
            g = dot_nn(high, fwd_hi[...]) + dot_nn(low, fwd_hi[...]) + dot_nn(high, fwd_lo[...])
            scaled = []
            for e in range(step):
                row = cnt[w, k + e : k + e + 1, :]
                piece = g[e * rows : (e + 1) * rows]
                scaled.append(jnp.concatenate([piece[:, :LANES] * row, piece[:, LANES:] * row], 1))
            high, low = split(jnp.concatenate(scaled, 0))
            q = dot_nn(high, bwd_hi[...]) + dot_nn(low, bwd_hi[...]) + dot_nn(high, bwd_lo[...])
            for e in range(step):
                c, s = tw_cos[k + e : k + e + 1, :], tw_sin[k + e : k + e + 1, :]
                piece = q[e * rows : (e + 1) * rows]
                re, im = piece[:, :LANES], piece[:, LANES:]
                br[k + e] = re * c - im * s
                bi[k + e] = re * s + im * c

        def last(g, c2):
            top = pl.ds(pl.multiple_of(g * 8, 8), 8)
            bot = pl.ds(pl.multiple_of(rows + g * 8, 8), 8)
            re, im = [], []
            for k in range(outer):
                re.append(br[k, top, :])
                im.append(bi[k, top, :])
            re, im = small_fft(re, im, 1.0)
            for a in range(outer):
                c, s = kc[w, a : a + 1, :], ks[w, a : a + 1, :]
                out[a, top, :] += re[a] * c + im[a] * s
                out[a, bot, :] += im[a] * c - re[a] * s
            return c2

        lax.fori_loop(0, groups, last, 0)
        return carry

    lax.fori_loop(0, 2 * planes, plane, 0)


def backward_kernel(
    scal, x, corr, tw_cos, tw_sin, block, window, line_hi, line_lo, out, acc, yr, yi, zr, zi, sems
):
    rows = zr.shape[0]
    outer = yr.shape[0]
    length = outer * LANES
    half = rows // 2
    groups = rows // 8
    acc[...] = jnp.zeros(acc.shape, F32)
    table_hi, table_lo = split(block[...] * window[...])
    for s in range(x.shape[0] // 2):
        re = jnp.concatenate([x[2 * s, 0:half, :], x[2 * s + 1, 0:half, :]], 0)
        im = jnp.concatenate([x[2 * s, half : 2 * half, :], x[2 * s + 1, half : 2 * half, :]], 0)
        high, low = split(turned_rows(re, im, half))
        z = dot_nt(table_hi, high) + dot_nt(table_hi, low) + dot_nt(table_lo, high)
        at = pl.ds(scal[1 + s], LANES)
        acc[at, :] = acc[at, :] + z
    acc[0:LANES, :] = acc[0:LANES, :] + acc[length : length + LANES, :]

    def second(k, carry):
        z = acc[pl.ds(k, LANES, stride=outer), :]
        high, low = split(z.T)
        p = dot_nn(high, line_hi[...]) + dot_nn(low, line_hi[...]) + dot_nn(high, line_lo[...])
        c, s = tw_cos[pl.ds(k, 1), :], tw_sin[pl.ds(k, 1), :]
        for h in range(2):
            a, b = p[2 * h * half : (2 * h + 1) * half], p[(2 * h + 1) * half : (2 * h + 2) * half]
            re = a[:, :LANES] - b[:, LANES:]
            im = a[:, LANES:] + b[:, :LANES]
            yr[k, h * half : (h + 1) * half, :] = re * c - im * s
            yi[k, h * half : (h + 1) * half, :] = re * s + im * c
        return carry

    lax.fori_loop(0, outer, second, 0)

    def copies(g):
        at = pl.ds(g * 8, 8)
        return (
            pltpu.make_async_copy(zr.at[at, :], out.at[at, 0, :], sems.at[0, g]),
            pltpu.make_async_copy(zi.at[at, :], out.at[at, 1, :], sems.at[1, g]),
        )

    def last(g, carry):
        at = pl.ds(pl.multiple_of(g * 8, 8), 8)
        re, im = [], []
        for k in range(outer):
            re.append(yr[k, at, :])
            im.append(yi[k, at, :])
        re, im = small_fft(re, im, 1.0)
        for a in range(outer):
            scale = corr[a : a + 1, :]
            lanes = pl.ds(a * LANES, LANES)
            zr[at, lanes] = re[a] * scale
            zi[at, lanes] = im[a] * scale
        for c in copies(g):
            c.start()
        return carry

    lax.fori_loop(0, groups, last, 0)
    for g in range(groups):
        for c in copies(g):
            c.wait()


VMEM_LIMIT = 60 * 1024 * 1024


def vmem():
    return pl.BlockSpec(memory_space=pltpu.VMEM)


def hbm():
    return pl.BlockSpec(memory_space=pl.ANY)


def params():
    return pltpu.CompilerParams(vmem_limit_bytes=VMEM_LIMIT)


def on_device(facets, correction, window, offsets, phases, coverage):
    sub_count = lax.axis_size("sub")
    pair_count = lax.axis_size("wa")
    facet_count = lax.axis_size("facet")
    sub = lax.axis_index("sub")
    pair = lax.axis_index("wa")
    facet = lax.axis_index("facet")
    length = facets.shape[3]
    outer = length // LANES
    rows = facets.shape[1] // (sub_count * pair_count)
    half = rows // 2
    per_owner = coverage.shape[0]
    subgrids = offsets.shape[0]
    width = facet_count * LANES

    turned = jnp.roll(offsets.reshape(sub_count, per_owner), -sub, axis=0).reshape(subgrids)
    scal = jnp.concatenate([((sub * pair_count + pair) * rows)[None], turned]).astype(jnp.int32)

    slot = facet // 2
    mine = lax.dynamic_index_in_dim(coverage, slot % per_owner, 0, keepdims=False).astype(F32)
    payload = jnp.concatenate([mine, phases], 0).reshape(-1, facet_count, LANES)
    names = ("facet", "sub", "wa")

    def number(f, y, w):
        return (f * sub_count + y) * pair_count + w

    def fetch(flip):
        route = []
        for f in range(facet_count):
            for y in range(sub_count):
                for w in range(pair_count):
                    source = (f, (y + f // 2 // per_owner) % sub_count, w ^ flip)
                    route.append((number(*source), number(f, y, w)))
        return lax.ppermute(payload, names, route)

    own, other = fetch(0), fetch(1)

    tw = trig(outer, LANES, length)
    tw_cos, tw_sin = jnp.asarray(tw[0], F32), jnp.asarray(tw[1], F32)
    c128, s128 = trig(LANES, LANES, LANES)
    corr = correction.reshape(outer, LANES)
    wide_hi, wide_lo = halves(np.concatenate([c128, s128], 1) * length**-0.5)
    cells = np.concatenate([c128, s128], 1) * LANES**-0.5

    sent = pl.pallas_call(
        forward_kernel,
        grid_spec=pltpu.PrefetchScalarGridSpec(
            num_scalar_prefetch=1,
            grid=(1,),
            in_specs=[hbm()] + [vmem()] * 7,
            out_specs=vmem(),
            scratch_shapes=[
                pltpu.VMEM((rows, length), F32),
                pltpu.VMEM((rows, length), F32),
                pltpu.VMEM((outer, rows, LANES), F32),
                pltpu.VMEM((outer, rows, LANES), F32),
                pltpu.VMEM((length + LANES, LANES), F32),
                pltpu.SemaphoreType.DMA((2, rows // 8)),
            ],
        ),
        out_shape=jax.ShapeDtypeStruct((facet_count, rows, LANES), F32),
        compiler_params=params(),
        name="forward",
    )(
        scal, facets.reshape(facets.shape[1:]), corr, tw_cos, tw_sin, wide_hi, wide_lo,
        jnp.asarray(cells, F32), window.reshape(LANES, 1),
    )
    got = lax.all_to_all(sent, "facet", split_axis=0, concat_axis=0, tiled=True)

    tw2 = trig(facet_count, LANES, width)
    fwd = np.block([[c128, -s128], [s128, c128]])
    fwd_hi, fwd_lo = halves(fwd)
    bwd_hi, bwd_lo = halves(np.block([[c128, s128], [-s128, c128]]) * (1.0 / (width * WPLANES)))
    adjoint = pl.pallas_call(
        middle_kernel,
        in_specs=[vmem()] * 9,
        out_specs=vmem(),
        scratch_shapes=[pltpu.VMEM((WPLANES, facet_count, LANES), F32)] * 3
        + [pltpu.VMEM((facet_count, half, LANES), F32)] * 2,
        out_shape=jax.ShapeDtypeStruct((facet_count, rows, LANES), F32),
        compiler_params=params(),
        name="middle",
    )(
        got, own, other, jnp.asarray(tw2[0], F32), jnp.asarray(tw2[1], F32), fwd_hi, fwd_lo, bwd_hi, bwd_lo
    )
    back = lax.all_to_all(adjoint, "facet", split_axis=0, concat_axis=0, tiled=True)

    result = pl.pallas_call(
        backward_kernel,
        grid_spec=pltpu.PrefetchScalarGridSpec(
            num_scalar_prefetch=1,
            grid=(1,),
            in_specs=[vmem()] * 8,
            out_specs=hbm(),
            scratch_shapes=[
                pltpu.VMEM((length + LANES, LANES), F32),
                pltpu.VMEM((outer, rows, LANES), F32),
                pltpu.VMEM((outer, rows, LANES), F32),
                pltpu.VMEM((rows, length), F32),
                pltpu.VMEM((rows, length), F32),
                pltpu.SemaphoreType.DMA((2, rows // 8)),
            ],
        ),
        out_shape=jax.ShapeDtypeStruct((rows, 2, length), F32),
        compiler_params=params(),
        name="backward",
    )(
        scal, back, corr, tw_cos, tw_sin, jnp.asarray(cells, F32), window.reshape(LANES, 1), wide_hi, wide_lo
    )
    return result.reshape(1, rows, 2, length)


def solution(mesh):
    return jax.shard_map(
        on_device,
        mesh=mesh,
        in_specs=(
            P("facet", None, None, None),
            P("facet", None),
            P(),
            P(),
            P("wa", None),
            P("sub", "wa", None),
        ),
        out_specs=P("facet", ("sub", "wa"), None, None),
        check_vma=False,
    )
```

```python
import math

import jax
import jax.numpy as jnp
import numpy as np
from jax import lax
from jax.experimental import pallas as pl
from jax.experimental.pallas import tpu as pltpu
from jax.sharding import PartitionSpec as P

WPLANES = 4
LANES = 128
F32 = jnp.float32
BF16 = jnp.bfloat16


def trig(rows, cols, length):
    product = np.arange(rows, dtype=np.int64)[:, None] * np.arange(cols, dtype=np.int64)[None, :]
    angle = (product % length) * (2.0 * math.pi / length)
    return np.cos(angle), np.sin(angle)


def np_halves(table):
    high = table.astype(np.float32).astype(BF16)
    low = (table - high.astype(np.float64)).astype(np.float32).astype(BF16)
    return high, low


def halves(table):
    high, low = np_halves(table)
    return jnp.asarray(high), jnp.asarray(low)


def split(x):
    high = x.astype(BF16)
    return high, (x - high.astype(F32)).astype(BF16)


def mul_const(re, im, c, s):
    tiny = 1e-12
    if abs(s) < tiny:
        return (re, im) if c > 0 else (-re, -im)
    if abs(c) < tiny:
        return (-im, re) if s > 0 else (im, -re)
    if abs(abs(c) - abs(s)) < tiny:
        u = re * c
        v = im * c
        return (u - v, u + v) if c * s > 0 else (u + v, v - u)
    return re * c - im * s, re * s + im * c


def small_fft(re, im, sign):
    n = len(re)
    if n == 1:
        return re, im
    radix = 4 if n % 4 == 0 else 2
    m = n // radix
    parts = [small_fft(re[j::radix], im[j::radix], sign) for j in range(radix)]
    out_re, out_im = [None] * n, [None] * n
    for k in range(m):
        terms = []
        for j in range(radix):
            angle = sign * 2.0 * math.pi * j * k / n
            terms.append(mul_const(parts[j][0][k], parts[j][1][k], math.cos(angle), math.sin(angle)))
        if radix == 2:
            (ar, ai), (br, bi) = terms
            out_re[k], out_im[k] = ar + br, ai + bi
            out_re[k + m], out_im[k + m] = ar - br, ai - bi
        else:
            (ar, ai), (br, bi), (cr, ci), (dr, di) = terms
            sr, si, tr, ti = ar + cr, ai + ci, ar - cr, ai - ci
            ur, ui, vr, vi = br + dr, bi + di, br - dr, bi - di
            out_re[k], out_im[k] = sr + ur, si + ui
            out_re[k + 2 * m], out_im[k + 2 * m] = sr - ur, si - ui
            if sign > 0:
                out_re[k + m], out_im[k + m] = tr - vi, ti + vr
                out_re[k + 3 * m], out_im[k + 3 * m] = tr + vi, ti - vr
            else:
                out_re[k + m], out_im[k + m] = tr + vi, ti - vr
                out_re[k + 3 * m], out_im[k + 3 * m] = tr - vi, ti + vr
    return out_re, out_im


def dot_nt(a, b):
    return lax.dot_general(a, b, (((1,), (1,)), ((), ())), preferred_element_type=F32)


def dot_nn(a, b):
    return lax.dot_general(a, b, (((1,), (0,)), ((), ())), preferred_element_type=F32)


def product(x, table_hi, table_lo):
    high, low = split(x)
    return dot_nn(high, table_hi) + dot_nn(low, table_hi) + dot_nn(high, table_lo)


def turned_rows(re, im, half):
    left, right = [], []
    for at in range(0, re.shape[0], half):
        a, b = re[at : at + half], im[at : at + half]
        left += [a, b]
        right += [b, -a]
    return jnp.concatenate([jnp.concatenate(left, 0), jnp.concatenate(right, 0)], 1)


def turned_halves(pairs, half):
    highs, lows = [], []
    for re, im in pairs:
        (rh, rl), (ih, il) = split(re), split(im)
        highs.append(turned_rows(rh, ih, half))
        lows.append(turned_rows(rl, il, half))
    return jnp.concatenate(highs, 0), jnp.concatenate(lows, 0)


def columns_product(table, table_hi, pairs, half):
    high, low = turned_halves(pairs, half)
    n = table_hi.shape[0]
    both = dot_nt(table, high)
    return both[:n] + both[n:] + dot_nt(table_hi, low)


def side_by_side(x, half):
    re = [x[at : at + half] for at in range(0, x.shape[0], 2 * half)]
    im = [x[at + half : at + 2 * half] for at in range(0, x.shape[0], 2 * half)]
    return jnp.concatenate([jnp.concatenate(re, 0), jnp.concatenate(im, 0)], 1)


PITCH = LANES + 16
FRONT = 8


def piece_row(offset, c, outer):
    at = offset + c
    shift = outer.bit_length() - 1
    return (at & (outer - 1)) * PITCH + (at >> shift) + FRONT


def window_column(window, outer):
    per = LANES // outer
    row = lax.broadcasted_iota(jnp.int32, (LANES, LANES), 0)
    lane = lax.broadcasted_iota(jnp.int32, (LANES, LANES), 1)
    wide = jnp.broadcast_to(window, (LANES, LANES))
    return jnp.sum(jnp.where(lane == row // per + outer * (row % per), wide, 0.0), axis=1, keepdims=True)


def slot_offset(offsets, slot, subs, per_owner):
    owner = (slot // per_owner + lax.axis_index("sub")) & (subs - 1)
    return offsets[owner * per_owner + slot % per_owner]


def forward_kernel(
    subs, pairs, per_owner, offsets, facets, corr_h, tw_h, line_h, block_h, window_h, out, xr, xi, yr, yi, spec, corr, tw, line,
    block, window, sems, table_sems
):
    rows = xr.shape[0]
    outer = yr.shape[0]
    half = rows // 2
    groups = rows // 8
    base = pl.multiple_of((lax.axis_index("sub") * pairs + lax.axis_index("wa")) * rows, rows)

    def copies(g):
        at = pl.ds(g * 8, 8)
        return (
            pltpu.make_async_copy(facets.at[pl.ds(base + g * 8, 8), 0, :], xr.at[at, :], sems.at[0, g]),
            pltpu.make_async_copy(facets.at[pl.ds(base + g * 8, 8), 1, :], xi.at[at, :], sems.at[1, g]),
        )

    pieces = ((corr_h, corr), (tw_h, tw), (line_h, line), (block_h, block), (window_h, window))
    tables = [pltpu.make_async_copy(src, dst, table_sems.at[i]) for i, (src, dst) in enumerate(pieces)]
    for c in tables[:2]:
        c.start()
    for g in range(groups):
        for c in copies(g):
            c.start()
    for c in tables[2:]:
        c.start()
    for c in tables[:2]:
        c.wait()

    def first(g, carry):
        for c in copies(g):
            c.wait()
        at = pl.ds(pl.multiple_of(g * 8, 8), 8)
        re, im = [], []
        for a in range(outer):
            scale = corr[a : a + 1, :]
            lanes = pl.ds(a * LANES, LANES)
            re.append(xr[at, lanes] * scale)
            im.append(xi[at, lanes] * scale)
        re, im = small_fft(re, im, -1.0)
        for k in range(outer):
            c, s = tw[k : k + 1, :], tw[outer + k : outer + k + 1, :]
            yr[k, at, :] = re[k] * c + im[k] * s
            yi[k, at, :] = im[k] * c - re[k] * s
        return carry

    lax.fori_loop(0, groups, first, 0)
    for c in tables[2:]:
        c.wait()

    def second(j, carry):
        z = columns_product(line[...], line[:LANES, :], [(yr[2 * j + e], yi[2 * j + e]) for e in range(2)], half)
        for e in range(2):
            at = pl.multiple_of((2 * j + e) * PITCH + FRONT, 8)
            spec[pl.ds(at, LANES), :] = z[:, e * LANES : (e + 1) * LANES]
            spec[pl.ds(at + LANES, 8), :] = z[0:8, e * LANES : (e + 1) * LANES]
        return carry

    lax.fori_loop(0, outer // 2, second, 0, unroll=2)
    top = block[...] * window_column(window[...], outer)
    bottom = jnp.concatenate([-top[:, LANES:], top[:, :LANES]], 1)
    table_hi, table_lo = split(jnp.concatenate([top, bottom], 0))
    near = lax.broadcasted_iota(jnp.int32, (8, LANES), 0) < 4
    slots = out.shape[0] // 2
    batch = 4
    for first_slot in range(0, slots, batch):
        stacked = []
        for slot in range(first_slot, first_slot + batch):
            offset = slot_offset(offsets, slot, subs, per_owner)
            pieces = []
            for c in range(0, outer, 2):
                even = spec[pl.ds(piece_row(offset, c, outer), 8), :]
                odd = spec[pl.ds(piece_row(offset, c + 1, outer) - 4, 8), :]
                pieces.append(jnp.where(near, even, odd))
            stacked.append(side_by_side(jnp.concatenate(pieces, 0).T, half))
        p = product(jnp.concatenate(stacked, 0), table_hi, table_lo)
        for e in range(batch):
            for h in range(2):
                at = (2 * e + h) * half
                out[2 * (first_slot + e) + h, 0:half, :] = p[at : at + half, :LANES]
                out[2 * (first_slot + e) + h, half : 2 * half, :] = p[at : at + half, LANES:]


def ready_kernel(own, other, out):
    planes, outer = own.shape[0] // 2, own.shape[1]
    per = LANES // outer
    row = lax.broadcasted_iota(jnp.int32, (LANES, LANES), 0)
    lane = lax.broadcasted_iota(jnp.int32, (LANES, LANES), 1)
    mask = (row // outer) == (lane % per)
    short_row = lax.broadcasted_iota(jnp.int32, (outer, LANES), 0)
    short_lane = lax.broadcasted_iota(jnp.int32, (outer, LANES), 1)
    spread = (short_lane // per == short_row).astype(F32).astype(BF16)
    fold = (short_lane % outer == short_row).astype(F32).astype(BF16)
    for src, at in ((own, 0), (other, planes)):
        for w in range(planes):
            wide = dot_nn(src[w].T.astype(BF16), spread)
            out[2, at + w] = dot_nn(fold, jnp.where(mask, wide, 0.0).astype(BF16))
            out[0, at + w] = jnp.cos(src[planes + w])
            out[1, at + w] = jnp.sin(src[planes + w])


def middle_kernel(x, ready, tw_cos, tw_sin, fwd_hi, fwd_lo, bwd_hi, bwd_lo, out, br, bi, qr, qi):
    outer = x.shape[0]
    rows = x.shape[1] // 2
    groups = rows // 8
    planes = ready.shape[1]
    parts = 2
    step = outer // parts

    def first(w, g):
        top, bot = slice(g * 8, g * 8 + 8), slice(rows + g * 8, rows + g * 8 + 8)
        re, im = [], []
        for a in range(outer):
            c, s = ready[0, w, a : a + 1, :], ready[1, w, a : a + 1, :]
            p, q = x[a, top, :], x[a, bot, :]
            re.append(p * c - q * s)
            im.append(p * s + q * c)
        re, im = small_fft(re, im, -1.0)
        for k in range(outer):
            c, s = tw_cos[k : k + 1, :], tw_sin[k : k + 1, :]
            br[w % 2, k, top, :] = re[k] * c + im[k] * s
            bi[w % 2, k, top, :] = im[k] * c - re[k] * s

    def last(w, g):
        top, bot = slice(g * 8, g * 8 + 8), slice(rows + g * 8, rows + g * 8 + 8)
        re = [qr[w % 2, k, top, :] for k in range(outer)]
        im = [qi[w % 2, k, top, :] for k in range(outer)]
        re, im = small_fft(re, im, 1.0)
        for a in range(outer):
            c, s = ready[0, w, a : a + 1, :], ready[1, w, a : a + 1, :]
            hr, hi = re[a] * c + im[a] * s, im[a] * c - re[a] * s
            if w == 0:
                out[a, top, :] = hr
                out[a, bot, :] = hi
            else:
                out[a, top, :] += hr
                out[a, bot, :] += hi

    def to_grid(w, part):
        at = range(part * step, (part + 1) * step)
        left = jnp.concatenate([br[w % 2, k] for k in at], 0)
        right = jnp.concatenate([bi[w % 2, k] for k in at], 0)
        return product(jnp.concatenate([left, right], 1), fwd_hi[...], fwd_lo[...])

    def from_grid(w, part, g):
        scaled = []
        for e in range(step):
            row = ready[2, w, part * step + e : part * step + e + 1, :]
            piece = g[e * rows : (e + 1) * rows]
            scaled.append(jnp.concatenate([piece[:, :LANES] * row, piece[:, LANES:] * row], 1))
        q = product(jnp.concatenate(scaled, 0), bwd_hi[...], bwd_lo[...])
        for e in range(step):
            k = part * step + e
            c, s = tw_cos[k : k + 1, :], tw_sin[k : k + 1, :]
            re, im = q[e * rows : (e + 1) * rows, :LANES], q[e * rows : (e + 1) * rows, LANES:]
            qr[w % 2, k] = re * c - im * s
            qi[w % 2, k] = re * s + im * c

    for g in range(groups):
        first(0, g)
    for w in range(planes):
        for part in range(parts):
            grid = to_grid(w, part)
            for g in range(part * groups // parts, (part + 1) * groups // parts):
                if w + 1 < planes:
                    first(w + 1, g)
            from_grid(w, part, grid)
            for g in range(part * groups // parts, (part + 1) * groups // parts):
                if w > 0:
                    last(w - 1, g)
    for g in range(groups):
        last(planes - 1, g)


def backward_kernel(
    subs, per_owner, offsets, x, corr, tw_cos, tw_sin, block, window, line_hi, line_lo, out, acc, yr, yi, zr, zi, sems
):
    rows = zr.shape[0]
    outer = yr.shape[0]
    half = rows // 2
    groups = rows // 8
    acc[...] = jnp.zeros(acc.shape, F32)
    table_hi, table_lo = split(block[...] * window_column(window[...], outer))
    table = jnp.concatenate([table_hi, table_lo], 0)
    near = lax.broadcasted_iota(jnp.int32, (8, LANES), 0) < 4
    slots = x.shape[0] // 2
    for first_slot in range(0, slots, 2):
        parts = []
        for slot in range(first_slot, first_slot + 2):
            re = jnp.concatenate([x[2 * slot, 0:half, :], x[2 * slot + 1, 0:half, :]], 0)
            im = jnp.concatenate([x[2 * slot, half : 2 * half, :], x[2 * slot + 1, half : 2 * half, :]], 0)
            parts.append((re, im))
        z = columns_product(table, table_hi, parts, half)
        for e in range(2):
            offset = slot_offset(offsets, first_slot + e, subs, per_owner)
            at, value = [], []
            for c in range(outer):
                block_rows = z[(c // 2) * 8 : (c // 2) * 8 + 8, e * LANES : (e + 1) * LANES]
                at.append(pl.ds(piece_row(offset, c, outer) - (c % 2) * 4, 8))
                keep = near if c % 2 == 0 else jnp.logical_not(near)
                value.append(acc[at[c], :] + jnp.where(keep, block_rows, 0.0))
            for c in range(outer):
                acc[at[c], :] = value[c]

    batch = 4

    def second(j, carry):
        stacked = []
        for e in range(batch):
            at = pl.multiple_of((batch * j + e) * PITCH + FRONT, 8)
            head = acc[pl.ds(at, 8), :] + acc[pl.ds(at + LANES, 8), :]
            z = jnp.concatenate([head, acc[pl.ds(at + 8, LANES - 8), :]], 0)
            stacked.append(side_by_side(z.T, half))
        p = product(jnp.concatenate(stacked, 0), line_hi[...], line_lo[...])
        for e in range(batch):
            k = batch * j + e
            c, s = tw_cos[pl.ds(k, 1), :], tw_sin[pl.ds(k, 1), :]
            re, im = p[e * rows : (e + 1) * rows, :LANES], p[e * rows : (e + 1) * rows, LANES:]
            yr[k] = re * c - im * s
            yi[k] = re * s + im * c
        return carry

    lax.fori_loop(0, outer // batch, second, 0)

    def copies(g):
        at = pl.ds(g * 8, 8)
        return (
            pltpu.make_async_copy(zr.at[at, :], out.at[at, 0, :], sems.at[0, g]),
            pltpu.make_async_copy(zi.at[at, :], out.at[at, 1, :], sems.at[1, g]),
        )

    def last(g, carry):
        at = pl.ds(pl.multiple_of(g * 8, 8), 8)
        re, im = [], []
        for k in range(outer):
            re.append(yr[k, at, :])
            im.append(yi[k, at, :])
        re, im = small_fft(re, im, 1.0)
        for a in range(outer):
            scale = corr[a : a + 1, :]
            lanes = pl.ds(a * LANES, LANES)
            zr[at, lanes] = re[a] * scale
            zi[at, lanes] = im[a] * scale
        for c in copies(g):
            c.start()
        return carry

    lax.fori_loop(0, groups, last, 0)
    for g in range(groups):
        for c in copies(g):
            c.wait()


MIB = 1024 * 1024


def vmem():
    return pl.BlockSpec(memory_space=pltpu.VMEM)


def hbm():
    return pl.BlockSpec(memory_space=pltpu.HBM)


def smem():
    return pl.BlockSpec(memory_space=pltpu.SMEM)


def params(mib):
    return pltpu.CompilerParams(vmem_limit_bytes=mib * MIB)


def cost(flops, nbytes):
    return pl.CostEstimate(flops=flops, bytes_accessed=nbytes, transcendentals=0)


def on_device(facets, correction, window, offsets, phases, coverage):
    sub_count = lax.axis_size("sub")
    pair_count = lax.axis_size("wa")
    facet_count = lax.axis_size("facet")
    facet = lax.axis_index("facet")
    length = facets.shape[3]
    outer = length // LANES
    rows = facets.shape[1] // (sub_count * pair_count)
    half = rows // 2
    per_owner = coverage.shape[0]
    width = facet_count * LANES


    slot = facet // 2
    mine = lax.dynamic_index_in_dim(coverage, slot % per_owner, 0, keepdims=False).astype(F32)
    payload = jnp.concatenate([mine, phases], 0).reshape(-1, facet_count, LANES)
    names = ("facet", "sub", "wa")

    def number(f, y, w):
        return (f * sub_count + y) * pair_count + w

    def fetch(flip):
        route = []
        for f in range(facet_count):
            for y in range(sub_count):
                for w in range(pair_count):
                    source = (f, (y + f // 2 // per_owner) % sub_count, w ^ flip)
                    route.append((number(*source), number(f, y, w)))
        return lax.ppermute(payload, names, route)

    own, other = fetch(0), fetch(1)
    ready = pl.pallas_call(
        ready_kernel,
        in_specs=[vmem()] * 2,
        out_specs=vmem(),
        out_shape=jax.ShapeDtypeStruct((3, WPLANES, facet_count, LANES), F32),
        compiler_params=params(4),
        cost_estimate=cost(10**7, 10**6),
        name="ready",
    )(own, other)

    tw = trig(outer, LANES, length)
    tw_cos, tw_sin = jnp.asarray(tw[0], F32), jnp.asarray(tw[1], F32)
    tw_both = jnp.asarray(np.concatenate(tw, 0), F32)
    c128, s128 = trig(LANES, LANES, LANES)
    corr = correction.reshape(outer, LANES)
    line = jnp.asarray(np.concatenate(np_halves(np.concatenate([c128, s128], 1) * length**-0.5), 0))
    per = LANES // outer
    order = np.array([m // per + outer * (m % per) for m in range(LANES)])
    block = jnp.asarray(np.concatenate([c128[order], s128[order]], 1) * LANES**-0.5, F32)
    window = window.reshape(1, LANES)

    sent = pl.pallas_call(
        lambda *refs: forward_kernel(sub_count, pair_count, per_owner, *refs),
        in_specs=[smem()] + [hbm()] * 6,
        out_specs=vmem(),
        scratch_shapes=[
            pltpu.VMEM((rows, length), F32),
            pltpu.VMEM((rows, length), F32),
            pltpu.VMEM((outer, rows, LANES), F32),
            pltpu.VMEM((outer, rows, LANES), F32),
            pltpu.VMEM((outer * PITCH, LANES), F32),
            pltpu.VMEM(corr.shape, F32),
            pltpu.VMEM((2 * outer, LANES), F32),
            pltpu.VMEM(line.shape, BF16),
            pltpu.VMEM(block.shape, F32),
            pltpu.VMEM(window.shape, F32),
            pltpu.SemaphoreType.DMA((2, rows // 8)),
            pltpu.SemaphoreType.DMA((5,)),
        ],
        out_shape=jax.ShapeDtypeStruct((facet_count, rows, LANES), F32),
        compiler_params=params(60),
        cost_estimate=cost(10**9, 10**7),
        name="forward",
    )(offsets, facets.reshape(facets.shape[1:]), corr, tw_both, line, block, window)
    got = lax.all_to_all(sent, "facet", split_axis=0, concat_axis=0, tiled=True)

    tw2 = trig(facet_count, LANES, width)
    fwd_hi, fwd_lo = halves(np.block([[c128, -s128], [s128, c128]]))
    inverse = np.block([[c128, s128], [-s128, c128]])
    bwd_hi, bwd_lo = halves(inverse * (1.0 / (width * WPLANES)))
    adjoint = pl.pallas_call(
        middle_kernel,
        in_specs=[vmem()] * 8,
        out_specs=vmem(),
        scratch_shapes=[pltpu.VMEM((2, facet_count, half, LANES), F32)] * 4,
        out_shape=jax.ShapeDtypeStruct((facet_count, rows, LANES), F32),
        compiler_params=params(12),
        cost_estimate=cost(10**9, 10**7),
        name="middle",
    )(got, ready, jnp.asarray(tw2[0], F32), jnp.asarray(tw2[1], F32), fwd_hi, fwd_lo, bwd_hi, bwd_lo)
    back = lax.all_to_all(adjoint, "facet", split_axis=0, concat_axis=0, tiled=True)

    line_hi, line_lo = halves(inverse * length**-0.5)
    result = pl.pallas_call(
        lambda *refs: backward_kernel(sub_count, per_owner, *refs),
        in_specs=[smem()] + [vmem()] * 8,
        out_specs=hbm(),
        scratch_shapes=[
            pltpu.VMEM((outer * PITCH, LANES), F32),
            pltpu.VMEM((outer, rows, LANES), F32),
            pltpu.VMEM((outer, rows, LANES), F32),
            pltpu.VMEM((rows, length), F32),
            pltpu.VMEM((rows, length), F32),
            pltpu.SemaphoreType.DMA((2, rows // 8)),
        ],
        out_shape=jax.ShapeDtypeStruct((rows, 2, length), F32),
        compiler_params=params(16),
        cost_estimate=cost(10**9, 10**7),
        name="backward",
    )(offsets, back, corr, tw_cos, tw_sin, block, window, line_hi, line_lo)
    return result.reshape(1, rows, 2, length)


def solution(mesh):
    return jax.shard_map(
        on_device,
        mesh=mesh,
        in_specs=(
            P("facet", None, None, None),
            P("facet", None),
            P(),
            P(),
            P("wa", None),
            P("sub", "wa", None),
        ),
        out_specs=P("facet", ("sub", "wa"), None, None),
        check_vma=False,
    )
```

```python
import math

import jax
import jax.numpy as jnp
import numpy as np
from jax import lax
from jax.experimental import pallas as pl
from jax.experimental.pallas import tpu as pltpu
from jax.sharding import PartitionSpec as P

WPLANES = 4
LANES = 128
F32 = jnp.float32
BF16 = jnp.bfloat16


def trig(rows, cols, length):
    product = np.arange(rows, dtype=np.int64)[:, None] * np.arange(cols, dtype=np.int64)[None, :]
    angle = (product % length) * (2.0 * math.pi / length)
    return np.cos(angle), np.sin(angle)


def np_halves(table):
    high = table.astype(np.float32).astype(BF16)
    low = (table - high.astype(np.float64)).astype(np.float32).astype(BF16)
    return high, low


def halves(table):
    high, low = np_halves(table)
    return jnp.asarray(high), jnp.asarray(low)


def split(x):
    high = x.astype(BF16)
    return high, (x - high.astype(F32)).astype(BF16)


def mul_const(re, im, c, s):
    tiny = 1e-12
    if abs(s) < tiny:
        return (re, im) if c > 0 else (-re, -im)
    if abs(c) < tiny:
        return (-im, re) if s > 0 else (im, -re)
    if abs(abs(c) - abs(s)) < tiny:
        u = re * c
        v = im * c
        return (u - v, u + v) if c * s > 0 else (u + v, v - u)
    return re * c - im * s, re * s + im * c


def small_fft(re, im, sign):
    n = len(re)
    if n == 1:
        return re, im
    radix = 4 if n % 4 == 0 else 2
    m = n // radix
    parts = [small_fft(re[j::radix], im[j::radix], sign) for j in range(radix)]
    out_re, out_im = [None] * n, [None] * n
    for k in range(m):
        terms = []
        for j in range(radix):
            angle = sign * 2.0 * math.pi * j * k / n
            terms.append(mul_const(parts[j][0][k], parts[j][1][k], math.cos(angle), math.sin(angle)))
        if radix == 2:
            (ar, ai), (br, bi) = terms
            out_re[k], out_im[k] = ar + br, ai + bi
            out_re[k + m], out_im[k + m] = ar - br, ai - bi
        else:
            (ar, ai), (br, bi), (cr, ci), (dr, di) = terms
            sr, si, tr, ti = ar + cr, ai + ci, ar - cr, ai - ci
            ur, ui, vr, vi = br + dr, bi + di, br - dr, bi - di
            out_re[k], out_im[k] = sr + ur, si + ui
            out_re[k + 2 * m], out_im[k + 2 * m] = sr - ur, si - ui
            if sign > 0:
                out_re[k + m], out_im[k + m] = tr - vi, ti + vr
                out_re[k + 3 * m], out_im[k + 3 * m] = tr + vi, ti - vr
            else:
                out_re[k + m], out_im[k + m] = tr + vi, ti - vr
                out_re[k + 3 * m], out_im[k + 3 * m] = tr - vi, ti + vr
    return out_re, out_im


def dot_nt(a, b):
    return lax.dot_general(a, b, (((1,), (1,)), ((), ())), preferred_element_type=F32)


def dot_nn(a, b):
    return lax.dot_general(a, b, (((1,), (0,)), ((), ())), preferred_element_type=F32)


def product(x, table_hi, table_lo):
    high, low = split(x)
    return dot_nn(high, table_hi) + dot_nn(low, table_hi) + dot_nn(high, table_lo)


def turned_rows(re, im, half):
    left, right = [], []
    for at in range(0, re.shape[0], half):
        a, b = re[at : at + half], im[at : at + half]
        left += [a, b]
        right += [b, -a]
    return jnp.concatenate([jnp.concatenate(left, 0), jnp.concatenate(right, 0)], 1)


def turned_halves(pairs, half):
    highs, lows = [], []
    for re, im in pairs:
        (rh, rl), (ih, il) = split(re), split(im)
        highs.append(turned_rows(rh, ih, half))
        lows.append(turned_rows(rl, il, half))
    return jnp.concatenate(highs, 0), jnp.concatenate(lows, 0)


def columns_product(table, table_hi, pairs, half):
    high, low = turned_halves(pairs, half)
    n = table_hi.shape[0]
    both = dot_nt(table, high)
    return both[:n] + both[n:] + dot_nt(table_hi, low)


def side_by_side(x, half):
    re = [x[at : at + half] for at in range(0, x.shape[0], 2 * half)]
    im = [x[at + half : at + 2 * half] for at in range(0, x.shape[0], 2 * half)]
    return jnp.concatenate([jnp.concatenate(re, 0), jnp.concatenate(im, 0)], 1)


PITCH = LANES + 16
FRONT = 8


def piece_row(offset, c, outer):
    at = offset + c
    shift = outer.bit_length() - 1
    return (at & (outer - 1)) * PITCH + (at >> shift) + FRONT


def window_column(window, outer):
    per = LANES // outer
    row = lax.broadcasted_iota(jnp.int32, (LANES, LANES), 0)
    lane = lax.broadcasted_iota(jnp.int32, (LANES, LANES), 1)
    wide = jnp.broadcast_to(window, (LANES, LANES))
    return jnp.sum(jnp.where(lane == row // per + outer * (row % per), wide, 0.0), axis=1, keepdims=True)


def slot_offset(offsets, slot, subs, per_owner):
    owner = (slot // per_owner + lax.axis_index("sub")) & (subs - 1)
    return offsets[owner * per_owner + slot % per_owner]


def forward_kernel(
    subs, pairs, per_owner, offsets, facets, corr_h, tw_h, line_h, block_h, window_h, out, xr, xi, yr, yi, spec, corr, tw, line,
    block, window, sems, table_sems
):
    rows = xr.shape[0]
    outer = yr.shape[0]
    half = rows // 2
    groups = rows // 8
    base = pl.multiple_of((lax.axis_index("sub") * pairs + lax.axis_index("wa")) * rows, rows)

    def copies(g):
        at = pl.ds(g * 8, 8)
        return (
            pltpu.make_async_copy(facets.at[pl.ds(base + g * 8, 8), 0, :], xr.at[at, :], sems.at[0, g]),
            pltpu.make_async_copy(facets.at[pl.ds(base + g * 8, 8), 1, :], xi.at[at, :], sems.at[1, g]),
        )

    pieces = ((corr_h, corr), (tw_h, tw), (line_h, line), (block_h, block), (window_h, window))
    tables = [pltpu.make_async_copy(src, dst, table_sems.at[i]) for i, (src, dst) in enumerate(pieces)]
    for c in tables[:2]:
        c.start()
    for g in range(groups):
        for c in copies(g):
            c.start()
    for c in tables[2:]:
        c.start()
    for c in tables[:2]:
        c.wait()

    def first(g, carry):
        for c in copies(g):
            c.wait()
        at = pl.ds(pl.multiple_of(g * 8, 8), 8)
        re, im = [], []
        for a in range(outer):
            scale = corr[a : a + 1, :]
            lanes = pl.ds(a * LANES, LANES)
            re.append(xr[at, lanes] * scale)
            im.append(xi[at, lanes] * scale)
        re, im = small_fft(re, im, -1.0)
        for k in range(outer):
            c, s = tw[k : k + 1, :], tw[outer + k : outer + k + 1, :]
            yr[k, at, :] = re[k] * c + im[k] * s
            yi[k, at, :] = im[k] * c - re[k] * s
        return carry

    lax.fori_loop(0, groups, first, 0)
    for c in tables[2:]:
        c.wait()

    def second(j, carry):
        z = columns_product(line[...], line[:LANES, :], [(yr[2 * j + e], yi[2 * j + e]) for e in range(2)], half)
        for e in range(2):
            at = pl.multiple_of((2 * j + e) * PITCH + FRONT, 8)
            spec[pl.ds(at, LANES), :] = z[:, e * LANES : (e + 1) * LANES]
            spec[pl.ds(at + LANES, 8), :] = z[0:8, e * LANES : (e + 1) * LANES]
        return carry

    lax.fori_loop(0, outer // 2, second, 0, unroll=2)
    top = block[...] * window_column(window[...], outer)
    bottom = jnp.concatenate([-top[:, LANES:], top[:, :LANES]], 1)
    table_hi, table_lo = split(jnp.concatenate([top, bottom], 0))
    near = lax.broadcasted_iota(jnp.int32, (8, LANES), 0) < 4
    slots = out.shape[0] // 2
    batch = 4
    for first_slot in range(0, slots, batch):
        stacked = []
        for slot in range(first_slot, first_slot + batch):
            offset = slot_offset(offsets, slot, subs, per_owner)
            pieces = []
            for c in range(0, outer, 2):
                even = spec[pl.ds(piece_row(offset, c, outer), 8), :]
                odd = spec[pl.ds(piece_row(offset, c + 1, outer) - 4, 8), :]
                pieces.append(jnp.where(near, even, odd))
            stacked.append(side_by_side(jnp.concatenate(pieces, 0).T, half))
        p = product(jnp.concatenate(stacked, 0), table_hi, table_lo)
        for e in range(batch):
            for h in range(2):
                at = (2 * e + h) * half
                out[2 * (first_slot + e) + h, 0:half, :] = p[at : at + half, :LANES]
                out[2 * (first_slot + e) + h, half : 2 * half, :] = p[at : at + half, LANES:]


def ready_kernel(own, other, out):
    planes, outer = own.shape[0] // 2, own.shape[1]
    per = LANES // outer
    row = lax.broadcasted_iota(jnp.int32, (LANES, LANES), 0)
    lane = lax.broadcasted_iota(jnp.int32, (LANES, LANES), 1)
    mask = (row // outer) == (lane % per)
    short_row = lax.broadcasted_iota(jnp.int32, (outer, LANES), 0)
    short_lane = lax.broadcasted_iota(jnp.int32, (outer, LANES), 1)
    spread = (short_lane // per == short_row).astype(F32).astype(BF16)
    fold = (short_lane % outer == short_row).astype(F32).astype(BF16)
    for src, at in ((own, 0), (other, planes)):
        for w in range(planes):
            wide = dot_nn(src[w].T.astype(BF16), spread)
            out[2, at + w] = dot_nn(fold, jnp.where(mask, wide, 0.0).astype(BF16))
            out[0, at + w] = jnp.cos(src[planes + w])
            out[1, at + w] = jnp.sin(src[planes + w])


def middle_kernel(x, ready, tw_cos, tw_sin, fwd_hi, fwd_lo, bwd_hi, bwd_lo, out, br, bi, qr, qi):
    outer = x.shape[0]
    rows = x.shape[1] // 2
    groups = rows // 8
    planes = ready.shape[1]
    parts = 2
    step = outer // parts

    def first(w, g):
        top, bot = slice(g * 8, g * 8 + 8), slice(rows + g * 8, rows + g * 8 + 8)
        re, im = [], []
        for a in range(outer):
            c, s = ready[0, w, a : a + 1, :], ready[1, w, a : a + 1, :]
            p, q = x[a, top, :], x[a, bot, :]
            re.append(p * c - q * s)
            im.append(p * s + q * c)
        re, im = small_fft(re, im, -1.0)
        for k in range(outer):
            c, s = tw_cos[k : k + 1, :], tw_sin[k : k + 1, :]
            br[w % 2, k, top, :] = re[k] * c + im[k] * s
            bi[w % 2, k, top, :] = im[k] * c - re[k] * s

    def last(w, g):
        top, bot = slice(g * 8, g * 8 + 8), slice(rows + g * 8, rows + g * 8 + 8)
        re = [qr[w % 2, k, top, :] for k in range(outer)]
        im = [qi[w % 2, k, top, :] for k in range(outer)]
        re, im = small_fft(re, im, 1.0)
        for a in range(outer):
            c, s = ready[0, w, a : a + 1, :], ready[1, w, a : a + 1, :]
            hr, hi = re[a] * c + im[a] * s, im[a] * c - re[a] * s
            if w == 0:
                out[a, top, :] = hr
                out[a, bot, :] = hi
            else:
                out[a, top, :] += hr
                out[a, bot, :] += hi

    def to_grid(w, part):
        at = range(part * step, (part + 1) * step)
        left = jnp.concatenate([br[w % 2, k] for k in at], 0)
        right = jnp.concatenate([bi[w % 2, k] for k in at], 0)
        return product(jnp.concatenate([left, right], 1), fwd_hi[...], fwd_lo[...])

    def from_grid(w, part, g):
        scaled = []
        for e in range(step):
            row = ready[2, w, part * step + e : part * step + e + 1, :]
            piece = g[e * rows : (e + 1) * rows]
            scaled.append(jnp.concatenate([piece[:, :LANES] * row, piece[:, LANES:] * row], 1))
        q = product(jnp.concatenate(scaled, 0), bwd_hi[...], bwd_lo[...])
        for e in range(step):
            k = part * step + e
            c, s = tw_cos[k : k + 1, :], tw_sin[k : k + 1, :]
            re, im = q[e * rows : (e + 1) * rows, :LANES], q[e * rows : (e + 1) * rows, LANES:]
            qr[w % 2, k] = re * c - im * s
            qi[w % 2, k] = re * s + im * c

    for g in range(groups):
        first(0, g)
    for w in range(planes):
        for part in range(parts):
            grid = to_grid(w, part)
            for g in range(part * groups // parts, (part + 1) * groups // parts):
                if w + 1 < planes:
                    first(w + 1, g)
            from_grid(w, part, grid)
            for g in range(part * groups // parts, (part + 1) * groups // parts):
                if w > 0:
                    last(w - 1, g)
    for g in range(groups):
        last(planes - 1, g)


def backward_kernel(
    subs, per_owner, offsets, x, corr, tw_cos, tw_sin, block, window, line_hi, line_lo, out, acc, yr, yi, zr, zi, sems
):
    rows = zr.shape[0]
    outer = yr.shape[0]
    half = rows // 2
    groups = rows // 8
    acc[...] = jnp.zeros(acc.shape, F32)
    table_hi, table_lo = split(block[...] * window_column(window[...], outer))
    table = jnp.concatenate([table_hi, table_lo], 0)
    near = lax.broadcasted_iota(jnp.int32, (8, LANES), 0) < 4
    slots = x.shape[0] // 2
    for first_slot in range(0, slots, 2):
        parts = []
        for slot in range(first_slot, first_slot + 2):
            re = jnp.concatenate([x[2 * slot, 0:half, :], x[2 * slot + 1, 0:half, :]], 0)
            im = jnp.concatenate([x[2 * slot, half : 2 * half, :], x[2 * slot + 1, half : 2 * half, :]], 0)
            parts.append((re, im))
        z = columns_product(table, table_hi, parts, half)
        for e in range(2):
            offset = slot_offset(offsets, first_slot + e, subs, per_owner)
            at, value = [], []
            for c in range(outer):
                block_rows = z[(c // 2) * 8 : (c // 2) * 8 + 8, e * LANES : (e + 1) * LANES]
                at.append(pl.ds(piece_row(offset, c, outer) - (c % 2) * 4, 8))
                keep = near if c % 2 == 0 else jnp.logical_not(near)
                value.append(acc[at[c], :] + jnp.where(keep, block_rows, 0.0))
            for c in range(outer):
                acc[at[c], :] = value[c]

    batch = 4

    def second(j, carry):
        stacked = []
        for e in range(batch):
            at = pl.multiple_of((batch * j + e) * PITCH + FRONT, 8)
            head = acc[pl.ds(at, 8), :] + acc[pl.ds(at + LANES, 8), :]
            z = jnp.concatenate([head, acc[pl.ds(at + 8, LANES - 8), :]], 0)
            stacked.append(side_by_side(z.T, half))
        p = product(jnp.concatenate(stacked, 0), line_hi[...], line_lo[...])
        for e in range(batch):
            k = batch * j + e
            c, s = tw_cos[pl.ds(k, 1), :], tw_sin[pl.ds(k, 1), :]
            re, im = p[e * rows : (e + 1) * rows, :LANES], p[e * rows : (e + 1) * rows, LANES:]
            yr[k] = re * c - im * s
            yi[k] = re * s + im * c
        return carry

    lax.fori_loop(0, outer // batch, second, 0)

    def copies(g):
        at = pl.ds(g * 8, 8)
        return (
            pltpu.make_async_copy(zr.at[at, :], out.at[at, 0, :], sems.at[0, g]),
            pltpu.make_async_copy(zi.at[at, :], out.at[at, 1, :], sems.at[1, g]),
        )

    def last(g, carry):
        at = pl.ds(pl.multiple_of(g * 8, 8), 8)
        re, im = [], []
        for k in range(outer):
            re.append(yr[k, at, :])
            im.append(yi[k, at, :])
        re, im = small_fft(re, im, 1.0)
        for a in range(outer):
            scale = corr[a : a + 1, :]
            lanes = pl.ds(a * LANES, LANES)
            zr[at, lanes] = re[a] * scale
            zi[at, lanes] = im[a] * scale
        for c in copies(g):
            c.start()
        return carry

    lax.fori_loop(0, groups, last, 0)
    for g in range(groups):
        for c in copies(g):
            c.wait()


MIB = 1024 * 1024


def vmem():
    return pl.BlockSpec(memory_space=pltpu.VMEM)


def hbm():
    return pl.BlockSpec(memory_space=pltpu.HBM)


def smem():
    return pl.BlockSpec(memory_space=pltpu.SMEM)


def params(mib):
    return pltpu.CompilerParams(vmem_limit_bytes=mib * MIB)


def cost(flops, nbytes):
    return pl.CostEstimate(flops=flops, bytes_accessed=nbytes, transcendentals=0)


def on_device(facets, correction, window, offsets, phases, coverage):
    sub_count = lax.axis_size("sub")
    pair_count = lax.axis_size("wa")
    facet_count = lax.axis_size("facet")
    facet = lax.axis_index("facet")
    length = facets.shape[3]
    outer = length // LANES
    rows = facets.shape[1] // (sub_count * pair_count)
    half = rows // 2
    per_owner = coverage.shape[0]
    width = facet_count * LANES


    slot = facet // 2
    mine = lax.dynamic_index_in_dim(coverage, slot % per_owner, 0, keepdims=False).astype(F32)
    payload = jnp.concatenate([mine, phases], 0).reshape(-1, facet_count, LANES)
    names = ("facet", "sub", "wa")

    def number(f, y, w):
        return (f * sub_count + y) * pair_count + w

    route = []
    for f in range(facet_count):
        for y in range(sub_count):
            for w in range(pair_count):
                source = (f, (y + f // 2 // per_owner) % sub_count, w ^ (f % 2))
                route.append((number(*source), number(f, y, w)))
    fetched = lax.ppermute(payload, names, route)
    swapped = lax.ppermute(fetched, "facet", [(f, f ^ 1) for f in range(facet_count)])
    ready = pl.pallas_call(
        ready_kernel,
        in_specs=[vmem()] * 2,
        out_specs=vmem(),
        out_shape=jax.ShapeDtypeStruct((3, WPLANES, facet_count, LANES), F32),
        compiler_params=params(4),
        cost_estimate=cost(10**7, 10**6),
        name="ready",
    )(fetched, swapped)

    tw = trig(outer, LANES, length)
    tw_cos, tw_sin = jnp.asarray(tw[0], F32), jnp.asarray(tw[1], F32)
    tw_both = jnp.asarray(np.concatenate(tw, 0), F32)
    c128, s128 = trig(LANES, LANES, LANES)
    corr = correction.reshape(outer, LANES)
    line = jnp.asarray(np.concatenate(np_halves(np.concatenate([c128, s128], 1) * length**-0.5), 0))
    per = LANES // outer
    order = np.array([m // per + outer * (m % per) for m in range(LANES)])
    block = jnp.asarray(np.concatenate([c128[order], s128[order]], 1) * LANES**-0.5, F32)
    window = window.reshape(1, LANES)

    sent = pl.pallas_call(
        lambda *refs: forward_kernel(sub_count, pair_count, per_owner, *refs),
        in_specs=[smem()] + [hbm()] * 6,
        out_specs=vmem(),
        scratch_shapes=[
            pltpu.VMEM((rows, length), F32),
            pltpu.VMEM((rows, length), F32),
            pltpu.VMEM((outer, rows, LANES), F32),
            pltpu.VMEM((outer, rows, LANES), F32),
            pltpu.VMEM((outer * PITCH, LANES), F32),
            pltpu.VMEM(corr.shape, F32),
            pltpu.VMEM((2 * outer, LANES), F32),
            pltpu.VMEM(line.shape, BF16),
            pltpu.VMEM(block.shape, F32),
            pltpu.VMEM(window.shape, F32),
            pltpu.SemaphoreType.DMA((2, rows // 8)),
            pltpu.SemaphoreType.DMA((5,)),
        ],
        out_shape=jax.ShapeDtypeStruct((facet_count, rows, LANES), F32),
        compiler_params=params(60),
        cost_estimate=cost(10**9, 10**7),
        name="forward",
    )(offsets, facets.reshape(facets.shape[1:]), corr, tw_both, line, block, window)
    got = lax.all_to_all(sent, "facet", split_axis=0, concat_axis=0, tiled=True)

    tw2 = trig(facet_count, LANES, width)
    fwd_hi, fwd_lo = halves(np.block([[c128, -s128], [s128, c128]]))
    inverse = np.block([[c128, s128], [-s128, c128]])
    bwd_hi, bwd_lo = halves(inverse * (1.0 / (width * WPLANES)))
    adjoint = pl.pallas_call(
        middle_kernel,
        in_specs=[vmem()] * 8,
        out_specs=vmem(),
        scratch_shapes=[pltpu.VMEM((2, facet_count, half, LANES), F32)] * 4,
        out_shape=jax.ShapeDtypeStruct((facet_count, rows, LANES), F32),
        compiler_params=params(12),
        cost_estimate=cost(10**9, 10**7),
        name="middle",
    )(got, ready, jnp.asarray(tw2[0], F32), jnp.asarray(tw2[1], F32), fwd_hi, fwd_lo, bwd_hi, bwd_lo)
    back = lax.all_to_all(adjoint, "facet", split_axis=0, concat_axis=0, tiled=True)

    line_hi, line_lo = halves(inverse * length**-0.5)
    result = pl.pallas_call(
        lambda *refs: backward_kernel(sub_count, per_owner, *refs),
        in_specs=[smem()] + [vmem()] * 8,
        out_specs=hbm(),
        scratch_shapes=[
            pltpu.VMEM((outer * PITCH, LANES), F32),
            pltpu.VMEM((outer, rows, LANES), F32),
            pltpu.VMEM((outer, rows, LANES), F32),
            pltpu.VMEM((rows, length), F32),
            pltpu.VMEM((rows, length), F32),
            pltpu.SemaphoreType.DMA((2, rows // 8)),
        ],
        out_shape=jax.ShapeDtypeStruct((rows, 2, length), F32),
        compiler_params=params(16),
        cost_estimate=cost(10**9, 10**7),
        name="backward",
    )(offsets, back, corr, tw_cos, tw_sin, block, window, line_hi, line_lo)
    return result.reshape(1, rows, 2, length)


def solution(mesh):
    return jax.shard_map(
        on_device,
        mesh=mesh,
        in_specs=(
            P("facet", None, None, None),
            P("facet", None),
            P(),
            P(),
            P("wa", None),
            P("sub", "wa", None),
        ),
        out_specs=P("facet", ("sub", "wa"), None, None),
        check_vma=False,
    )
```

```python
import math

import jax
import jax.numpy as jnp
import numpy as np
from jax import lax
from jax.experimental import pallas as pl
from jax.experimental.pallas import tpu as pltpu
from jax.sharding import PartitionSpec as P

WPLANES = 4
LANES = 128
F32 = jnp.float32
BF16 = jnp.bfloat16


def trig(rows, cols, length):
    product = np.arange(rows, dtype=np.int64)[:, None] * np.arange(cols, dtype=np.int64)[None, :]
    angle = (product % length) * (2.0 * math.pi / length)
    return np.cos(angle), np.sin(angle)


def np_halves(table):
    high = table.astype(np.float32).astype(BF16)
    low = (table - high.astype(np.float64)).astype(np.float32).astype(BF16)
    return high, low


def halves(table):
    high, low = np_halves(table)
    return jnp.asarray(high), jnp.asarray(low)


def split(x):
    high = x.astype(BF16)
    return high, (x - high.astype(F32)).astype(BF16)


def mul_const(re, im, c, s):
    tiny = 1e-12
    if abs(s) < tiny:
        return (re, im) if c > 0 else (-re, -im)
    if abs(c) < tiny:
        return (-im, re) if s > 0 else (im, -re)
    if abs(abs(c) - abs(s)) < tiny:
        u = re * c
        v = im * c
        return (u - v, u + v) if c * s > 0 else (u + v, v - u)
    return re * c - im * s, re * s + im * c


def small_fft(re, im, sign):
    n = len(re)
    if n == 1:
        return re, im
    radix = 4 if n % 4 == 0 else 2
    m = n // radix
    parts = [small_fft(re[j::radix], im[j::radix], sign) for j in range(radix)]
    out_re, out_im = [None] * n, [None] * n
    for k in range(m):
        terms = []
        for j in range(radix):
            angle = sign * 2.0 * math.pi * j * k / n
            terms.append(mul_const(parts[j][0][k], parts[j][1][k], math.cos(angle), math.sin(angle)))
        if radix == 2:
            (ar, ai), (br, bi) = terms
            out_re[k], out_im[k] = ar + br, ai + bi
            out_re[k + m], out_im[k + m] = ar - br, ai - bi
        else:
            (ar, ai), (br, bi), (cr, ci), (dr, di) = terms
            sr, si, tr, ti = ar + cr, ai + ci, ar - cr, ai - ci
            ur, ui, vr, vi = br + dr, bi + di, br - dr, bi - di
            out_re[k], out_im[k] = sr + ur, si + ui
            out_re[k + 2 * m], out_im[k + 2 * m] = sr - ur, si - ui
            if sign > 0:
                out_re[k + m], out_im[k + m] = tr - vi, ti + vr
                out_re[k + 3 * m], out_im[k + 3 * m] = tr + vi, ti - vr
            else:
                out_re[k + m], out_im[k + m] = tr + vi, ti - vr
                out_re[k + 3 * m], out_im[k + 3 * m] = tr - vi, ti + vr
    return out_re, out_im


def dot_nn(a, b):
    return lax.dot_general(a, b, (((1,), (0,)), ((), ())), preferred_element_type=F32)


def product(x, table_hi, table_lo):
    high, low = split(x)
    return dot_nn(high, table_hi) + dot_nn(low, table_hi) + dot_nn(high, table_lo)


def side_by_side(x, half):
    re = [x[at : at + half] for at in range(0, x.shape[0], 2 * half)]
    im = [x[at + half : at + 2 * half] for at in range(0, x.shape[0], 2 * half)]
    return jnp.concatenate([jnp.concatenate(re, 0), jnp.concatenate(im, 0)], 1)


def one_below_other(x, half):
    parts = []
    for at in range(0, x.shape[0], half):
        parts += [x[at : at + half, :LANES], x[at : at + half, LANES:]]
    return jnp.concatenate(parts, 0)


PITCH = LANES + 16
FRONT = 8


def piece_row(offset, c, outer):
    at = offset + c
    shift = outer.bit_length() - 1
    return (at & (outer - 1)) * PITCH + (at >> shift) + FRONT


def window_column(window, outer):
    per = LANES // outer
    row = lax.broadcasted_iota(jnp.int32, (LANES, LANES), 0)
    lane = lax.broadcasted_iota(jnp.int32, (LANES, LANES), 1)
    wide = jnp.broadcast_to(window, (LANES, LANES))
    return jnp.sum(jnp.where(lane == row // per + outer * (row % per), wide, 0.0), axis=1, keepdims=True)


def slot_offset(offsets, slot, subs, per_owner):
    owner = (slot // per_owner + lax.axis_index("sub")) & (subs - 1)
    return offsets[owner * per_owner + slot % per_owner]


def forward_kernel(
    subs, pairs, per_owner, offsets, facets, corr_h, tw_h, line_h, block_h, window_h, out_h, xr, xi, yr, yi, spec, corr, tw, line,
    block, window, out, sems, table_sems, out_sems
):
    rows = xr.shape[0]
    outer = yr.shape[0]
    half = rows // 2
    groups = rows // 8
    base = pl.multiple_of((lax.axis_index("sub") * pairs + lax.axis_index("wa")) * rows, rows)

    def copies(g):
        at = pl.ds(g * 8, 8)
        return (
            pltpu.make_async_copy(facets.at[pl.ds(base + g * 8, 8), 0, :], xr.at[at, :], sems.at[0, g]),
            pltpu.make_async_copy(facets.at[pl.ds(base + g * 8, 8), 1, :], xi.at[at, :], sems.at[1, g]),
        )

    pieces = ((corr_h, corr), (tw_h, tw), (line_h, line), (block_h, block), (window_h, window))
    tables = [pltpu.make_async_copy(src, dst, table_sems.at[i]) for i, (src, dst) in enumerate(pieces)]
    for c in tables[:2]:
        c.start()
    for g in range(groups):
        for c in copies(g):
            c.start()
    for c in tables[2:]:
        c.start()
    for c in tables[:2]:
        c.wait()

    def first(g, carry):
        for c in copies(g):
            c.wait()
        at = pl.ds(pl.multiple_of(g * 8, 8), 8)
        re, im = [], []
        for a in range(outer):
            scale = corr[a : a + 1, :]
            lanes = pl.ds(a * LANES, LANES)
            re.append(xr[at, lanes] * scale)
            im.append(xi[at, lanes] * scale)
        re, im = small_fft(re, im, -1.0)
        for k in range(outer):
            c, s = tw[k : k + 1, :], tw[outer + k : outer + k + 1, :]
            yr[k, at, :] = re[k] * c + im[k] * s
            yi[k, at, :] = im[k] * c - re[k] * s
        return carry

    lax.fori_loop(0, groups, first, 0)
    for c in tables[2:]:
        c.wait()

    per_step = 8
    for j in range(outer // per_step):
        ks = range(j * per_step, (j + 1) * per_step)
        left = jnp.concatenate([yr[k] for k in ks], 0)
        right = jnp.concatenate([yi[k] for k in ks], 0)
        p = product(jnp.concatenate([left, right], 1), line[0], line[1])
        for e, k in enumerate(ks):
            z = one_below_other(p[e * rows : (e + 1) * rows], half).T
            spec[k * PITCH + FRONT : k * PITCH + FRONT + LANES, :] = z
            spec[k * PITCH + FRONT + LANES : k * PITCH + FRONT + LANES + 8, :] = z[0:8]
    top = block[...] * window_column(window[...], outer)
    bottom = jnp.concatenate([-top[:, LANES:], top[:, :LANES]], 1)
    table_hi, table_lo = split(jnp.concatenate([top, bottom], 0))
    near = lax.broadcasted_iota(jnp.int32, (8, LANES), 0) < 4
    slots = out.shape[0] // 2
    batch = 2
    sends = []
    for first_slot in range(0, slots, batch):
        stacked = []
        for slot in range(first_slot, first_slot + batch):
            offset = slot_offset(offsets, slot, subs, per_owner)
            pieces = []
            for c in range(0, outer, 2):
                even = spec[pl.ds(piece_row(offset, c, outer), 8), :]
                odd = spec[pl.ds(piece_row(offset, c + 1, outer) - 4, 8), :]
                pieces.append(jnp.where(near, even, odd))
            stacked.append(side_by_side(jnp.concatenate(pieces, 0).T, half))
        p = product(jnp.concatenate(stacked, 0), table_hi, table_lo)
        for e in range(batch):
            for h in range(2):
                at = (2 * e + h) * half
                out[2 * (first_slot + e) + h, 0:half, :] = p[at : at + half, :LANES]
                out[2 * (first_slot + e) + h, half : 2 * half, :] = p[at : at + half, LANES:]
        blocks = pl.ds(2 * first_slot, 2 * batch)
        sends.append(pltpu.make_async_copy(out.at[blocks], out_h.at[blocks], out_sems.at[first_slot // batch]))
        sends[-1].start()
    for c in sends:
        c.wait()


def ready_kernel(own, other, out):
    planes, outer = own.shape[0] // 2, own.shape[1]
    per = LANES // outer
    row = lax.broadcasted_iota(jnp.int32, (LANES, LANES), 0)
    lane = lax.broadcasted_iota(jnp.int32, (LANES, LANES), 1)
    mask = (row // outer) == (lane % per)
    short_row = lax.broadcasted_iota(jnp.int32, (outer, LANES), 0)
    short_lane = lax.broadcasted_iota(jnp.int32, (outer, LANES), 1)
    spread = (short_lane // per == short_row).astype(F32).astype(BF16)
    fold = (short_lane % outer == short_row).astype(F32).astype(BF16)
    for src, at in ((own, 0), (other, planes)):
        for w in range(planes):
            wide = dot_nn(src[w].T.astype(BF16), spread)
            out[2, at + w] = dot_nn(fold, jnp.where(mask, wide, 0.0).astype(BF16))
            out[0, at + w] = jnp.cos(src[planes + w])
            out[1, at + w] = jnp.sin(src[planes + w])


def middle_kernel(x, ready, tw_cos, tw_sin, fwd_hi, fwd_lo, bwd_hi, bwd_lo, out, br, bi, qr, qi):
    outer = x.shape[0]
    rows = x.shape[1] // 2
    groups = rows // 8
    planes = ready.shape[1]
    parts = 2
    step = outer // parts

    def first(w, g):
        top, bot = slice(g * 8, g * 8 + 8), slice(rows + g * 8, rows + g * 8 + 8)
        re, im = [], []
        for a in range(outer):
            c, s = ready[0, w, a : a + 1, :], ready[1, w, a : a + 1, :]
            p, q = x[a, top, :], x[a, bot, :]
            re.append(p * c - q * s)
            im.append(p * s + q * c)
        re, im = small_fft(re, im, -1.0)
        for k in range(outer):
            c, s = tw_cos[k : k + 1, :], tw_sin[k : k + 1, :]
            br[w % 2, k, top, :] = re[k] * c + im[k] * s
            bi[w % 2, k, top, :] = im[k] * c - re[k] * s

    def last(w, g):
        top, bot = slice(g * 8, g * 8 + 8), slice(rows + g * 8, rows + g * 8 + 8)
        re = [qr[w % 2, k, top, :] for k in range(outer)]
        im = [qi[w % 2, k, top, :] for k in range(outer)]
        re, im = small_fft(re, im, 1.0)
        for a in range(outer):
            c, s = ready[0, w, a : a + 1, :], ready[1, w, a : a + 1, :]
            hr, hi = re[a] * c + im[a] * s, im[a] * c - re[a] * s
            if w == 0:
                out[a, top, :] = hr
                out[a, bot, :] = hi
            else:
                out[a, top, :] += hr
                out[a, bot, :] += hi

    def to_grid(w, part):
        at = range(part * step, (part + 1) * step)
        left = jnp.concatenate([br[w % 2, k] for k in at], 0)
        right = jnp.concatenate([bi[w % 2, k] for k in at], 0)
        return product(jnp.concatenate([left, right], 1), fwd_hi[...], fwd_lo[...])

    def from_grid(w, part, g):
        scaled = []
        for e in range(step):
            row = ready[2, w, part * step + e : part * step + e + 1, :]
            piece = g[e * rows : (e + 1) * rows]
            scaled.append(jnp.concatenate([piece[:, :LANES] * row, piece[:, LANES:] * row], 1))
        q = product(jnp.concatenate(scaled, 0), bwd_hi[...], bwd_lo[...])
        for e in range(step):
            k = part * step + e
            c, s = tw_cos[k : k + 1, :], tw_sin[k : k + 1, :]
            re, im = q[e * rows : (e + 1) * rows, :LANES], q[e * rows : (e + 1) * rows, LANES:]
            qr[w % 2, k] = re * c - im * s
            qi[w % 2, k] = re * s + im * c

    for g in range(groups):
        first(0, g)
    for w in range(planes):
        for part in range(parts):
            grid = to_grid(w, part)
            for g in range(part * groups // parts, (part + 1) * groups // parts):
                if w + 1 < planes:
                    first(w + 1, g)
            from_grid(w, part, grid)
            for g in range(part * groups // parts, (part + 1) * groups // parts):
                if w > 0:
                    last(w - 1, g)
    for g in range(groups):
        last(planes - 1, g)


def backward_kernel(
    subs, per_owner, offsets, x, corr, tw_cos, tw_sin, block, window, line_hi, line_lo, out, acc, yr, yi, zr, zi, sems
):
    rows = zr.shape[0]
    outer = yr.shape[0]
    half = rows // 2
    groups = rows // 8
    acc[...] = jnp.zeros(acc.shape, F32)
    scale = jnp.broadcast_to(window_column(window[...], outer), (LANES, LANES)).T
    cos, sin = block[:, :LANES] * scale, block[:, LANES:] * scale
    top, bottom = jnp.concatenate([cos, -sin], 1), jnp.concatenate([sin, cos], 1)
    table_hi, table_lo = split(jnp.concatenate([top, bottom], 0))
    near = lax.broadcasted_iota(jnp.int32, (8, LANES), 0) < 4
    slots = x.shape[0] // 2
    group = 4
    for first_slot in range(0, slots, group):
        blocks = range(2 * first_slot, 2 * (first_slot + group))
        re = jnp.concatenate([x[d, 0:half, :] for d in blocks], 0)
        im = jnp.concatenate([x[d, half : 2 * half, :] for d in blocks], 0)
        p = product(jnp.concatenate([re, im], 1), table_hi, table_lo)
        for e in range(group):
            z = one_below_other(p[e * rows : (e + 1) * rows], half).T
            offset = slot_offset(offsets, first_slot + e, subs, per_owner)
            at, value = [], []
            for c in range(outer):
                block_rows = z[(c // 2) * 8 : (c // 2) * 8 + 8]
                at.append(pl.ds(piece_row(offset, c, outer) - (c % 2) * 4, 8))
                keep = near if c % 2 == 0 else jnp.logical_not(near)
                value.append(acc[at[c], :] + jnp.where(keep, block_rows, 0.0))
            for c in range(outer):
                acc[at[c], :] = value[c]

    batch = 4

    def second(j, carry):
        stacked = []
        for e in range(batch):
            at = pl.multiple_of((batch * j + e) * PITCH + FRONT, 8)
            head = acc[pl.ds(at, 8), :] + acc[pl.ds(at + LANES, 8), :]
            z = jnp.concatenate([head, acc[pl.ds(at + 8, LANES - 8), :]], 0)
            stacked.append(side_by_side(z.T, half))
        p = product(jnp.concatenate(stacked, 0), line_hi[...], line_lo[...])
        for e in range(batch):
            k = batch * j + e
            c, s = tw_cos[pl.ds(k, 1), :], tw_sin[pl.ds(k, 1), :]
            re, im = p[e * rows : (e + 1) * rows, :LANES], p[e * rows : (e + 1) * rows, LANES:]
            yr[k] = re * c - im * s
            yi[k] = re * s + im * c
        return carry

    lax.fori_loop(0, outer // batch, second, 0, unroll=outer // batch)

    def copies(g):
        at = pl.ds(g * 8, 8)
        return (
            pltpu.make_async_copy(zr.at[at, :], out.at[at, 0, :], sems.at[0, g]),
            pltpu.make_async_copy(zi.at[at, :], out.at[at, 1, :], sems.at[1, g]),
        )

    def last(g, carry):
        at = pl.ds(pl.multiple_of(g * 8, 8), 8)
        re, im = [], []
        for k in range(outer):
            re.append(yr[k, at, :])
            im.append(yi[k, at, :])
        re, im = small_fft(re, im, 1.0)
        for a in range(outer):
            scale = corr[a : a + 1, :]
            lanes = pl.ds(a * LANES, LANES)
            zr[at, lanes] = re[a] * scale
            zi[at, lanes] = im[a] * scale
        for c in copies(g):
            c.start()
        return carry

    lax.fori_loop(0, groups, last, 0)
    for g in range(groups):
        for c in copies(g):
            c.wait()


MIB = 1024 * 1024


def vmem():
    return pl.BlockSpec(memory_space=pltpu.VMEM)


def hbm():
    return pl.BlockSpec(memory_space=pltpu.HBM)


def smem():
    return pl.BlockSpec(memory_space=pltpu.SMEM)


def params(mib):
    return pltpu.CompilerParams(vmem_limit_bytes=mib * MIB)


def cost(flops, nbytes):
    return pl.CostEstimate(flops=flops, bytes_accessed=nbytes, transcendentals=0)


def on_device(facets, correction, window, offsets, phases, coverage):
    sub_count = lax.axis_size("sub")
    pair_count = lax.axis_size("wa")
    facet_count = lax.axis_size("facet")
    facet = lax.axis_index("facet")
    length = facets.shape[3]
    outer = length // LANES
    rows = facets.shape[1] // (sub_count * pair_count)
    half = rows // 2
    per_owner = coverage.shape[0]
    width = facet_count * LANES


    slot = facet // 2
    mine = lax.dynamic_index_in_dim(coverage, slot % per_owner, 0, keepdims=False).astype(F32)
    payload = jnp.concatenate([mine, phases], 0).reshape(-1, facet_count, LANES)
    names = ("facet", "sub", "wa")

    def number(f, y, w):
        return (f * sub_count + y) * pair_count + w

    route = []
    for f in range(facet_count):
        for y in range(sub_count):
            for w in range(pair_count):
                source = (f, (y + f // 2 // per_owner) % sub_count, w ^ (f % 2))
                route.append((number(*source), number(f, y, w)))
    fetched = lax.ppermute(payload, names, route)
    swapped = lax.ppermute(fetched, "facet", [(f, f ^ 1) for f in range(facet_count)])
    ready = pl.pallas_call(
        ready_kernel,
        in_specs=[vmem()] * 2,
        out_specs=vmem(),
        out_shape=jax.ShapeDtypeStruct((3, WPLANES, facet_count, LANES), F32),
        compiler_params=params(4),
        cost_estimate=cost(10**7, 10**6),
        name="ready",
    )(fetched, swapped)

    tw = trig(outer, LANES, length)
    tw_cos, tw_sin = jnp.asarray(tw[0], F32), jnp.asarray(tw[1], F32)
    tw_both = jnp.asarray(np.concatenate(tw, 0), F32)
    c128, s128 = trig(LANES, LANES, LANES)
    corr = correction.reshape(outer, LANES)
    line = jnp.asarray(np.stack(np_halves(np.block([[c128, -s128], [s128, c128]]) * length**-0.5)))
    per = LANES // outer
    order = np.array([m // per + outer * (m % per) for m in range(LANES)])
    block = jnp.asarray(np.concatenate([c128[order], s128[order]], 1) * LANES**-0.5, F32)
    back_block = jnp.asarray(np.concatenate([c128[:, order], s128[:, order]], 1) * LANES**-0.5, F32)
    window = window.reshape(1, LANES)

    sent = pl.pallas_call(
        lambda *refs: forward_kernel(sub_count, pair_count, per_owner, *refs),
        in_specs=[smem()] + [hbm()] * 6,
        out_specs=hbm(),
        scratch_shapes=[
            pltpu.VMEM((rows, length), F32),
            pltpu.VMEM((rows, length), F32),
            pltpu.VMEM((outer, rows, LANES), F32),
            pltpu.VMEM((outer, rows, LANES), F32),
            pltpu.VMEM((outer * PITCH, LANES), F32),
            pltpu.VMEM(corr.shape, F32),
            pltpu.VMEM((2 * outer, LANES), F32),
            pltpu.VMEM(line.shape, BF16),
            pltpu.VMEM(block.shape, F32),
            pltpu.VMEM(window.shape, F32),
            pltpu.VMEM((facet_count, rows, LANES), F32),
            pltpu.SemaphoreType.DMA((2, rows // 8)),
            pltpu.SemaphoreType.DMA((5,)),
            pltpu.SemaphoreType.DMA((facet_count // 4,)),
        ],
        out_shape=jax.ShapeDtypeStruct((facet_count, rows, LANES), F32),
        compiler_params=params(60),
        cost_estimate=cost(10**9, 10**7),
        name="forward",
    )(offsets, facets.reshape(facets.shape[1:]), corr, tw_both, line, block, window)
    got = lax.all_to_all(sent, "facet", split_axis=0, concat_axis=0, tiled=True)

    tw2 = trig(facet_count, LANES, width)
    fwd_hi, fwd_lo = halves(np.block([[c128, -s128], [s128, c128]]))
    inverse = np.block([[c128, s128], [-s128, c128]])
    bwd_hi, bwd_lo = halves(inverse * (1.0 / (width * WPLANES)))
    adjoint = pl.pallas_call(
        middle_kernel,
        in_specs=[vmem()] * 8,
        out_specs=vmem(),
        scratch_shapes=[pltpu.VMEM((2, facet_count, half, LANES), F32)] * 4,
        out_shape=jax.ShapeDtypeStruct((facet_count, rows, LANES), F32),
        compiler_params=params(12),
        cost_estimate=cost(10**9, 10**7),
        name="middle",
    )(got, ready, jnp.asarray(tw2[0], F32), jnp.asarray(tw2[1], F32), fwd_hi, fwd_lo, bwd_hi, bwd_lo)
    back = lax.all_to_all(adjoint, "facet", split_axis=0, concat_axis=0, tiled=True)

    line_hi, line_lo = halves(inverse * length**-0.5)
    result = pl.pallas_call(
        lambda *refs: backward_kernel(sub_count, per_owner, *refs),
        in_specs=[smem()] + [vmem()] * 8,
        out_specs=hbm(),
        scratch_shapes=[
            pltpu.VMEM((outer * PITCH, LANES), F32),
            pltpu.VMEM((outer, rows, LANES), F32),
            pltpu.VMEM((outer, rows, LANES), F32),
            pltpu.VMEM((rows, length), F32),
            pltpu.VMEM((rows, length), F32),
            pltpu.SemaphoreType.DMA((2, rows // 8)),
        ],
        out_shape=jax.ShapeDtypeStruct((rows, 2, length), F32),
        compiler_params=params(16),
        cost_estimate=cost(10**9, 10**7),
        name="backward",
    )(offsets, back, corr, tw_cos, tw_sin, back_block, window, line_hi, line_lo)
    return result.reshape(1, rows, 2, length)


def solution(mesh):
    return jax.shard_map(
        on_device,
        mesh=mesh,
        in_specs=(
            P("facet", None, None, None),
            P("facet", None),
            P(),
            P(),
            P("wa", None),
            P("sub", "wa", None),
        ),
        out_specs=P("facet", ("sub", "wa"), None, None),
        check_vma=False,
    )
```

```python
import math

import jax
import jax.numpy as jnp
import numpy as np
from jax import lax
from jax.experimental import pallas as pl
from jax.experimental.pallas import tpu as pltpu
from jax.sharding import PartitionSpec as P

WPLANES = 4
LANES = 128
F32 = jnp.float32
BF16 = jnp.bfloat16


def trig(rows, cols, length):
    product = np.arange(rows, dtype=np.int64)[:, None] * np.arange(cols, dtype=np.int64)[None, :]
    angle = (product % length) * (2.0 * math.pi / length)
    return np.cos(angle), np.sin(angle)


def np_halves(table):
    high = table.astype(np.float32).astype(BF16)
    low = (table - high.astype(np.float64)).astype(np.float32).astype(BF16)
    return high, low


def halves(table):
    high, low = np_halves(table)
    return jnp.asarray(high), jnp.asarray(low)


def split(x):
    high = x.astype(BF16)
    return high, (x - high.astype(F32)).astype(BF16)


def mul_const(re, im, c, s):
    tiny = 1e-12
    if abs(s) < tiny:
        return (re, im) if c > 0 else (-re, -im)
    if abs(c) < tiny:
        return (-im, re) if s > 0 else (im, -re)
    if abs(abs(c) - abs(s)) < tiny:
        u = re * c
        v = im * c
        return (u - v, u + v) if c * s > 0 else (u + v, v - u)
    return re * c - im * s, re * s + im * c


def small_fft(re, im, sign):
    n = len(re)
    if n == 1:
        return re, im
    radix = 4 if n % 4 == 0 else 2
    m = n // radix
    parts = [small_fft(re[j::radix], im[j::radix], sign) for j in range(radix)]
    out_re, out_im = [None] * n, [None] * n
    for k in range(m):
        terms = []
        for j in range(radix):
            angle = sign * 2.0 * math.pi * j * k / n
            terms.append(mul_const(parts[j][0][k], parts[j][1][k], math.cos(angle), math.sin(angle)))
        if radix == 2:
            (ar, ai), (br, bi) = terms
            out_re[k], out_im[k] = ar + br, ai + bi
            out_re[k + m], out_im[k + m] = ar - br, ai - bi
        else:
            (ar, ai), (br, bi), (cr, ci), (dr, di) = terms
            sr, si, tr, ti = ar + cr, ai + ci, ar - cr, ai - ci
            ur, ui, vr, vi = br + dr, bi + di, br - dr, bi - di
            out_re[k], out_im[k] = sr + ur, si + ui
            out_re[k + 2 * m], out_im[k + 2 * m] = sr - ur, si - ui
            if sign > 0:
                out_re[k + m], out_im[k + m] = tr - vi, ti + vr
                out_re[k + 3 * m], out_im[k + 3 * m] = tr + vi, ti - vr
            else:
                out_re[k + m], out_im[k + m] = tr + vi, ti - vr
                out_re[k + 3 * m], out_im[k + 3 * m] = tr - vi, ti + vr
    return out_re, out_im


def dot_nn(a, b):
    return lax.dot_general(a, b, (((1,), (0,)), ((), ())), preferred_element_type=F32)


def product(x, table_hi, table_lo):
    high, low = split(x)
    return dot_nn(high, table_hi) + dot_nn(low, table_hi) + dot_nn(high, table_lo)


def side_by_side(x, half):
    re = [x[at : at + half] for at in range(0, x.shape[0], 2 * half)]
    im = [x[at + half : at + 2 * half] for at in range(0, x.shape[0], 2 * half)]
    return jnp.concatenate([jnp.concatenate(re, 0), jnp.concatenate(im, 0)], 1)


def one_below_other(x, half):
    parts = []
    for at in range(0, x.shape[0], half):
        parts += [x[at : at + half, :LANES], x[at : at + half, LANES:]]
    return jnp.concatenate(parts, 0)


PITCH = LANES + 16
FRONT = 8


def piece_row(offset, c, outer):
    at = offset + c
    shift = outer.bit_length() - 1
    return (at & (outer - 1)) * PITCH + (at >> shift) + FRONT


def window_column(window, outer):
    per = LANES // outer
    row = lax.broadcasted_iota(jnp.int32, (LANES, LANES), 0)
    lane = lax.broadcasted_iota(jnp.int32, (LANES, LANES), 1)
    wide = jnp.broadcast_to(window, (LANES, LANES))
    return jnp.sum(jnp.where(lane == row // per + outer * (row % per), wide, 0.0), axis=1, keepdims=True)


def slot_offset(offsets, slot, subs, per_owner):
    owner = (slot // per_owner + lax.axis_index("sub")) & (subs - 1)
    return offsets[owner * per_owner + slot % per_owner]


def forward_kernel(
    subs, pairs, per_owner, place, offsets, facets, corr_h, tw_h, line_h, block_h, window_h, out_h, xr, xi, yr, yi, spec, corr, tw, line,
    block, window, out, sems, table_sems, out_sems
):
    rows = xr.shape[0]
    outer = yr.shape[0]
    half = rows // 2
    groups = rows // 8
    base = pl.multiple_of((lax.axis_index("sub") * pairs + lax.axis_index("wa")) * rows, rows)

    def copies(g):
        at = pl.ds(g * 8, 8)
        return (
            pltpu.make_async_copy(facets.at[pl.ds(base + g * 8, 8), 0, :], xr.at[at, :], sems.at[0, g]),
            pltpu.make_async_copy(facets.at[pl.ds(base + g * 8, 8), 1, :], xi.at[at, :], sems.at[1, g]),
        )

    pieces = ((corr_h, corr), (tw_h, tw), (line_h, line), (block_h, block), (window_h, window))
    tables = [pltpu.make_async_copy(src, dst, table_sems.at[i]) for i, (src, dst) in enumerate(pieces)]
    for c in tables[:2]:
        c.start()
    for g in range(groups):
        for c in copies(g):
            c.start()
    for c in tables[2:]:
        c.start()
    for c in tables[:2]:
        c.wait()

    def first(g, carry):
        for c in copies(g):
            c.wait()
        at = pl.ds(pl.multiple_of(g * 8, 8), 8)
        re, im = [], []
        for a in range(outer):
            scale = corr[a : a + 1, :]
            lanes = pl.ds(a * LANES, LANES)
            re.append(xr[at, lanes] * scale)
            im.append(xi[at, lanes] * scale)
        re, im = small_fft(re, im, -1.0)
        for k in range(outer):
            c, s = tw[k : k + 1, :], tw[outer + k : outer + k + 1, :]
            yr[k, at, :] = re[k] * c + im[k] * s
            yi[k, at, :] = im[k] * c - re[k] * s
        return carry

    lax.fori_loop(0, groups, first, 0)
    for c in tables[2:]:
        c.wait()

    per_step = 8
    for j in range(outer // per_step):
        ks = range(j * per_step, (j + 1) * per_step)
        left = jnp.concatenate([yr[k] for k in ks], 0)
        right = jnp.concatenate([yi[k] for k in ks], 0)
        p = product(jnp.concatenate([left, right], 1), line[0], line[1])
        for e, k in enumerate(ks):
            z = one_below_other(p[e * rows : (e + 1) * rows], half).T
            spec[k * PITCH + FRONT : k * PITCH + FRONT + LANES, :] = z
            spec[k * PITCH + FRONT + LANES : k * PITCH + FRONT + LANES + 8, :] = z[0:8]
    top = block[...] * window_column(window[...], outer)
    bottom = jnp.concatenate([-top[:, LANES:], top[:, :LANES]], 1)
    table_hi, table_lo = split(jnp.concatenate([top, bottom], 0))
    near = lax.broadcasted_iota(jnp.int32, (8, LANES), 0) < 4
    slots = out.shape[0] // 2
    batch = 2
    sends = []
    for first_slot in range(0, slots, batch):
        stacked = []
        for slot in range(first_slot, first_slot + batch):
            offset = slot_offset(offsets, slot, subs, per_owner)
            pieces = []
            for c in range(0, outer, 2):
                even = spec[pl.ds(piece_row(offset, c, outer), 8), :]
                odd = spec[pl.ds(piece_row(offset, c + 1, outer) - 4, 8), :]
                pieces.append(jnp.where(near, even, odd))
            stacked.append(side_by_side(jnp.concatenate(pieces, 0).T, half))
        p = product(jnp.concatenate(stacked, 0), table_hi, table_lo)
        for e in range(batch):
            for h in range(2):
                at = (2 * e + h) * half
                to = place[2 * (first_slot + e) + h]
                out[to, 0:half, :] = p[at : at + half, :LANES]
                out[to, half : 2 * half, :] = p[at : at + half, LANES:]
                sends.append(pltpu.make_async_copy(out.at[to], out_h.at[to], out_sems.at[to]))
                sends[-1].start()
    for c in sends:
        c.wait()


def ready_kernel(own, other, out):
    planes, outer = own.shape[0] // 2, own.shape[1]
    per = LANES // outer
    row = lax.broadcasted_iota(jnp.int32, (LANES, LANES), 0)
    lane = lax.broadcasted_iota(jnp.int32, (LANES, LANES), 1)
    mask = (row // outer) == (lane % per)
    short_row = lax.broadcasted_iota(jnp.int32, (outer, LANES), 0)
    short_lane = lax.broadcasted_iota(jnp.int32, (outer, LANES), 1)
    spread = (short_lane // per == short_row).astype(F32).astype(BF16)
    fold = (short_lane % outer == short_row).astype(F32).astype(BF16)
    for src, at in ((own, 0), (other, planes)):
        for w in range(planes):
            wide = dot_nn(src[w].T.astype(BF16), spread)
            out[2, at + w] = dot_nn(fold, jnp.where(mask, wide, 0.0).astype(BF16))
            out[0, at + w] = jnp.cos(src[planes + w])
            out[1, at + w] = jnp.sin(src[planes + w])


def middle_kernel(place, x, ready, tw_cos, tw_sin, fwd_hi, fwd_lo, bwd_hi, bwd_lo, out, br, bi, qr, qi):
    outer = x.shape[0]
    rows = x.shape[1] // 2
    groups = rows // 8
    planes = ready.shape[1]
    parts = 2
    step = outer // parts

    def first(w, g):
        top, bot = slice(g * 8, g * 8 + 8), slice(rows + g * 8, rows + g * 8 + 8)
        re, im = [], []
        for a in range(outer):
            c, s = ready[0, w, a : a + 1, :], ready[1, w, a : a + 1, :]
            p, q = x[place[a], top, :], x[place[a], bot, :]
            re.append(p * c - q * s)
            im.append(p * s + q * c)
        re, im = small_fft(re, im, -1.0)
        for k in range(outer):
            c, s = tw_cos[k : k + 1, :], tw_sin[k : k + 1, :]
            br[w % 2, k, top, :] = re[k] * c + im[k] * s
            bi[w % 2, k, top, :] = im[k] * c - re[k] * s

    def last(w, g):
        top, bot = slice(g * 8, g * 8 + 8), slice(rows + g * 8, rows + g * 8 + 8)
        re = [qr[w % 2, k, top, :] for k in range(outer)]
        im = [qi[w % 2, k, top, :] for k in range(outer)]
        re, im = small_fft(re, im, 1.0)
        for a in range(outer):
            c, s = ready[0, w, a : a + 1, :], ready[1, w, a : a + 1, :]
            hr, hi = re[a] * c + im[a] * s, im[a] * c - re[a] * s
            to = place[a]
            if w == 0:
                out[to, top, :] = hr
                out[to, bot, :] = hi
            else:
                out[to, top, :] += hr
                out[to, bot, :] += hi

    def to_grid(w, part):
        at = range(part * step, (part + 1) * step)
        left = jnp.concatenate([br[w % 2, k] for k in at], 0)
        right = jnp.concatenate([bi[w % 2, k] for k in at], 0)
        return product(jnp.concatenate([left, right], 1), fwd_hi[...], fwd_lo[...])

    def from_grid(w, part, g):
        scaled = []
        for e in range(step):
            row = ready[2, w, part * step + e : part * step + e + 1, :]
            piece = g[e * rows : (e + 1) * rows]
            scaled.append(jnp.concatenate([piece[:, :LANES] * row, piece[:, LANES:] * row], 1))
        q = product(jnp.concatenate(scaled, 0), bwd_hi[...], bwd_lo[...])
        for e in range(step):
            k = part * step + e
            c, s = tw_cos[k : k + 1, :], tw_sin[k : k + 1, :]
            re, im = q[e * rows : (e + 1) * rows, :LANES], q[e * rows : (e + 1) * rows, LANES:]
            qr[w % 2, k] = re * c - im * s
            qi[w % 2, k] = re * s + im * c

    for g in range(groups):
        first(0, g)
    for w in range(planes):
        for part in range(parts):
            grid = to_grid(w, part)
            for g in range(part * groups // parts, (part + 1) * groups // parts):
                if w + 1 < planes:
                    first(w + 1, g)
            from_grid(w, part, grid)
            for g in range(part * groups // parts, (part + 1) * groups // parts):
                if w > 0:
                    last(w - 1, g)
    for g in range(groups):
        last(planes - 1, g)


def backward_kernel(
    subs, per_owner, place, offsets, x, corr, tw_cos, tw_sin, block, window, line_hi, line_lo, out, acc, yr, yi, zr, zi, sems
):
    rows = zr.shape[0]
    outer = yr.shape[0]
    half = rows // 2
    groups = rows // 8
    acc[...] = jnp.zeros(acc.shape, F32)
    scale = jnp.broadcast_to(window_column(window[...], outer), (LANES, LANES)).T
    cos, sin = block[:, :LANES] * scale, block[:, LANES:] * scale
    top, bottom = jnp.concatenate([cos, -sin], 1), jnp.concatenate([sin, cos], 1)
    table_hi, table_lo = split(jnp.concatenate([top, bottom], 0))
    near = lax.broadcasted_iota(jnp.int32, (8, LANES), 0) < 4
    slots = x.shape[0] // 2
    group = 4
    for first_slot in range(0, slots, group):
        blocks = [place[d] for d in range(2 * first_slot, 2 * (first_slot + group))]
        re = jnp.concatenate([x[d, 0:half, :] for d in blocks], 0)
        im = jnp.concatenate([x[d, half : 2 * half, :] for d in blocks], 0)
        p = product(jnp.concatenate([re, im], 1), table_hi, table_lo)
        for e in range(group):
            z = one_below_other(p[e * rows : (e + 1) * rows], half).T
            offset = slot_offset(offsets, first_slot + e, subs, per_owner)
            at, value = [], []
            for c in range(outer):
                block_rows = z[(c // 2) * 8 : (c // 2) * 8 + 8]
                at.append(pl.ds(piece_row(offset, c, outer) - (c % 2) * 4, 8))
                keep = near if c % 2 == 0 else jnp.logical_not(near)
                value.append(acc[at[c], :] + jnp.where(keep, block_rows, 0.0))
            for c in range(outer):
                acc[at[c], :] = value[c]

    batch = 4

    def second(j, carry):
        stacked = []
        for e in range(batch):
            at = pl.multiple_of((batch * j + e) * PITCH + FRONT, 8)
            head = acc[pl.ds(at, 8), :] + acc[pl.ds(at + LANES, 8), :]
            z = jnp.concatenate([head, acc[pl.ds(at + 8, LANES - 8), :]], 0)
            stacked.append(side_by_side(z.T, half))
        p = product(jnp.concatenate(stacked, 0), line_hi[...], line_lo[...])
        for e in range(batch):
            k = batch * j + e
            c, s = tw_cos[pl.ds(k, 1), :], tw_sin[pl.ds(k, 1), :]
            re, im = p[e * rows : (e + 1) * rows, :LANES], p[e * rows : (e + 1) * rows, LANES:]
            yr[k] = re * c - im * s
            yi[k] = re * s + im * c
        return carry

    lax.fori_loop(0, outer // batch, second, 0, unroll=outer // batch)

    def copies(g):
        at = pl.ds(g * 8, 8)
        return (
            pltpu.make_async_copy(zr.at[at, :], out.at[at, 0, :], sems.at[0, g]),
            pltpu.make_async_copy(zi.at[at, :], out.at[at, 1, :], sems.at[1, g]),
        )

    def last(g, carry):
        at = pl.ds(pl.multiple_of(g * 8, 8), 8)
        re, im = [], []
        for k in range(outer):
            re.append(yr[k, at, :])
            im.append(yi[k, at, :])
        re, im = small_fft(re, im, 1.0)
        for a in range(outer):
            scale = corr[a : a + 1, :]
            lanes = pl.ds(a * LANES, LANES)
            zr[at, lanes] = re[a] * scale
            zi[at, lanes] = im[a] * scale
        for c in copies(g):
            c.start()
        return carry

    lax.fori_loop(0, groups, last, 0)
    for g in range(groups):
        for c in copies(g):
            c.wait()


MIB = 1024 * 1024


def vmem():
    return pl.BlockSpec(memory_space=pltpu.VMEM)


def hbm():
    return pl.BlockSpec(memory_space=pltpu.HBM)


def smem():
    return pl.BlockSpec(memory_space=pltpu.SMEM)


def params(mib):
    return pltpu.CompilerParams(vmem_limit_bytes=mib * MIB)


def cost(flops, nbytes):
    return pl.CostEstimate(flops=flops, bytes_accessed=nbytes, transcendentals=0)


def exchange_order(count):
    return list(range(count - 1, -1, -1))


def on_device(facets, correction, window, offsets, phases, coverage):
    sub_count = lax.axis_size("sub")
    pair_count = lax.axis_size("wa")
    facet_count = lax.axis_size("facet")
    facet = lax.axis_index("facet")
    length = facets.shape[3]
    outer = length // LANES
    rows = facets.shape[1] // (sub_count * pair_count)
    half = rows // 2
    per_owner = coverage.shape[0]
    width = facet_count * LANES

    members = exchange_order(facet_count)
    place = [members.index(f) for f in range(facet_count)]

    def exchange(blocks):
        return lax.all_to_all(blocks, "facet", split_axis=0, concat_axis=0, tiled=True, axis_index_groups=[members])


    slot = facet // 2
    mine = lax.dynamic_index_in_dim(coverage, slot % per_owner, 0, keepdims=False).astype(F32)
    payload = jnp.concatenate([mine, phases], 0).reshape(-1, facet_count, LANES)
    names = ("facet", "sub", "wa")

    def number(f, y, w):
        return (f * sub_count + y) * pair_count + w

    route = []
    for f in range(facet_count):
        for y in range(sub_count):
            for w in range(pair_count):
                source = (f, (y + f // 2 // per_owner) % sub_count, w ^ (f % 2))
                route.append((number(*source), number(f, y, w)))
    fetched = lax.ppermute(payload, names, route)
    swapped = lax.ppermute(fetched, "facet", [(f, f ^ 1) for f in range(facet_count)])
    ready = pl.pallas_call(
        ready_kernel,
        in_specs=[vmem()] * 2,
        out_specs=vmem(),
        out_shape=jax.ShapeDtypeStruct((3, WPLANES, facet_count, LANES), F32),
        compiler_params=params(4),
        cost_estimate=cost(10**7, 10**6),
        name="ready",
    )(fetched, swapped)

    tw = trig(outer, LANES, length)
    tw_cos, tw_sin = jnp.asarray(tw[0], F32), jnp.asarray(tw[1], F32)
    tw_both = jnp.asarray(np.concatenate(tw, 0), F32)
    c128, s128 = trig(LANES, LANES, LANES)
    corr = correction.reshape(outer, LANES)
    line = jnp.asarray(np.stack(np_halves(np.block([[c128, -s128], [s128, c128]]) * length**-0.5)))
    per = LANES // outer
    order = np.array([m // per + outer * (m % per) for m in range(LANES)])
    block = jnp.asarray(np.concatenate([c128[order], s128[order]], 1) * LANES**-0.5, F32)
    back_block = jnp.asarray(np.concatenate([c128[:, order], s128[:, order]], 1) * LANES**-0.5, F32)
    window = window.reshape(1, LANES)

    sent = pl.pallas_call(
        lambda *refs: forward_kernel(sub_count, pair_count, per_owner, place, *refs),
        in_specs=[smem()] + [hbm()] * 6,
        out_specs=hbm(),
        scratch_shapes=[
            pltpu.VMEM((rows, length), F32),
            pltpu.VMEM((rows, length), F32),
            pltpu.VMEM((outer, rows, LANES), F32),
            pltpu.VMEM((outer, rows, LANES), F32),
            pltpu.VMEM((outer * PITCH, LANES), F32),
            pltpu.VMEM(corr.shape, F32),
            pltpu.VMEM((2 * outer, LANES), F32),
            pltpu.VMEM(line.shape, BF16),
            pltpu.VMEM(block.shape, F32),
            pltpu.VMEM(window.shape, F32),
            pltpu.VMEM((facet_count, rows, LANES), F32),
            pltpu.SemaphoreType.DMA((2, rows // 8)),
            pltpu.SemaphoreType.DMA((5,)),
            pltpu.SemaphoreType.DMA((facet_count,)),
        ],
        out_shape=jax.ShapeDtypeStruct((facet_count, rows, LANES), F32),
        compiler_params=params(60),
        cost_estimate=cost(10**9, 10**7),
        name="forward",
    )(offsets, facets.reshape(facets.shape[1:]), corr, tw_both, line, block, window)
    got = exchange(sent)

    tw2 = trig(facet_count, LANES, width)
    fwd_hi, fwd_lo = halves(np.block([[c128, -s128], [s128, c128]]))
    inverse = np.block([[c128, s128], [-s128, c128]])
    bwd_hi, bwd_lo = halves(inverse * (1.0 / (width * WPLANES)))
    adjoint = pl.pallas_call(
        lambda *refs: middle_kernel(place, *refs),
        in_specs=[vmem()] * 8,
        out_specs=vmem(),
        scratch_shapes=[pltpu.VMEM((2, facet_count, half, LANES), F32)] * 4,
        out_shape=jax.ShapeDtypeStruct((facet_count, rows, LANES), F32),
        compiler_params=params(12),
        cost_estimate=cost(10**9, 10**7),
        name="middle",
    )(got, ready, jnp.asarray(tw2[0], F32), jnp.asarray(tw2[1], F32), fwd_hi, fwd_lo, bwd_hi, bwd_lo)
    back = exchange(adjoint)

    line_hi, line_lo = halves(inverse * length**-0.5)
    result = pl.pallas_call(
        lambda *refs: backward_kernel(sub_count, per_owner, place, *refs),
        in_specs=[smem()] + [vmem()] * 8,
        out_specs=hbm(),
        scratch_shapes=[
            pltpu.VMEM((outer * PITCH, LANES), F32),
            pltpu.VMEM((outer, rows, LANES), F32),
            pltpu.VMEM((outer, rows, LANES), F32),
            pltpu.VMEM((rows, length), F32),
            pltpu.VMEM((rows, length), F32),
            pltpu.SemaphoreType.DMA((2, rows // 8)),
        ],
        out_shape=jax.ShapeDtypeStruct((rows, 2, length), F32),
        compiler_params=params(16),
        cost_estimate=cost(10**9, 10**7),
        name="backward",
    )(offsets, back, corr, tw_cos, tw_sin, back_block, window, line_hi, line_lo)
    return result.reshape(1, rows, 2, length)


def solution(mesh):
    return jax.shard_map(
        on_device,
        mesh=mesh,
        in_specs=(
            P("facet", None, None, None),
            P("facet", None),
            P(),
            P(),
            P("wa", None),
            P("sub", "wa", None),
        ),
        out_specs=P("facet", ("sub", "wa"), None, None),
        check_vma=False,
    )
```

```python
import math

import jax
import jax.numpy as jnp
import numpy as np
from jax import lax
from jax.experimental import pallas as pl
from jax.experimental.pallas import tpu as pltpu
from jax.sharding import PartitionSpec as P

WPLANES = 4
LANES = 128
F32 = jnp.float32
BF16 = jnp.bfloat16


def trig(rows, cols, length):
    product = np.arange(rows, dtype=np.int64)[:, None] * np.arange(cols, dtype=np.int64)[None, :]
    angle = (product % length) * (2.0 * math.pi / length)
    return np.cos(angle), np.sin(angle)


def np_halves(table):
    high = table.astype(np.float32).astype(BF16)
    low = (table - high.astype(np.float64)).astype(np.float32).astype(BF16)
    return high, low


def halves(table):
    high, low = np_halves(table)
    return jnp.asarray(high), jnp.asarray(low)


def split(x):
    high = x.astype(BF16)
    return high, (x - high.astype(F32)).astype(BF16)


def mul_const(re, im, c, s):
    tiny = 1e-12
    if abs(s) < tiny:
        return (re, im) if c > 0 else (-re, -im)
    if abs(c) < tiny:
        return (-im, re) if s > 0 else (im, -re)
    if abs(abs(c) - abs(s)) < tiny:
        u = re * c
        v = im * c
        return (u - v, u + v) if c * s > 0 else (u + v, v - u)
    return re * c - im * s, re * s + im * c


def small_fft(re, im, sign):
    n = len(re)
    if n == 1:
        return re, im
    radix = 4 if n % 4 == 0 else 2
    m = n // radix
    parts = [small_fft(re[j::radix], im[j::radix], sign) for j in range(radix)]
    out_re, out_im = [None] * n, [None] * n
    for k in range(m):
        terms = []
        for j in range(radix):
            angle = sign * 2.0 * math.pi * j * k / n
            terms.append(mul_const(parts[j][0][k], parts[j][1][k], math.cos(angle), math.sin(angle)))
        if radix == 2:
            (ar, ai), (br, bi) = terms
            out_re[k], out_im[k] = ar + br, ai + bi
            out_re[k + m], out_im[k + m] = ar - br, ai - bi
        else:
            (ar, ai), (br, bi), (cr, ci), (dr, di) = terms
            sr, si, tr, ti = ar + cr, ai + ci, ar - cr, ai - ci
            ur, ui, vr, vi = br + dr, bi + di, br - dr, bi - di
            out_re[k], out_im[k] = sr + ur, si + ui
            out_re[k + 2 * m], out_im[k + 2 * m] = sr - ur, si - ui
            if sign > 0:
                out_re[k + m], out_im[k + m] = tr - vi, ti + vr
                out_re[k + 3 * m], out_im[k + 3 * m] = tr + vi, ti - vr
            else:
                out_re[k + m], out_im[k + m] = tr + vi, ti - vr
                out_re[k + 3 * m], out_im[k + 3 * m] = tr - vi, ti + vr
    return out_re, out_im


def dot_nn(a, b):
    return lax.dot_general(a, b, (((1,), (0,)), ((), ())), preferred_element_type=F32)


def product(x, table_hi, table_lo):
    high, low = split(x)
    return dot_nn(high, table_hi) + dot_nn(low, table_hi) + dot_nn(high, table_lo)


def side_by_side(x, half):
    re = [x[at : at + half] for at in range(0, x.shape[0], 2 * half)]
    im = [x[at + half : at + 2 * half] for at in range(0, x.shape[0], 2 * half)]
    return jnp.concatenate([jnp.concatenate(re, 0), jnp.concatenate(im, 0)], 1)


def one_below_other(x, half):
    parts = []
    for at in range(0, x.shape[0], half):
        parts += [x[at : at + half, :LANES], x[at : at + half, LANES:]]
    return jnp.concatenate(parts, 0)


PITCH = LANES + 16
FRONT = 8


def piece_row(offset, c, outer):
    at = offset + c
    shift = outer.bit_length() - 1
    return (at & (outer - 1)) * PITCH + (at >> shift) + FRONT


def window_column(window, outer):
    per = LANES // outer
    row = lax.broadcasted_iota(jnp.int32, (LANES, LANES), 0)
    lane = lax.broadcasted_iota(jnp.int32, (LANES, LANES), 1)
    wide = jnp.broadcast_to(window, (LANES, LANES))
    return jnp.sum(jnp.where(lane == row // per + outer * (row % per), wide, 0.0), axis=1, keepdims=True)


def slot_offset(offsets, slot, subs, per_owner):
    owner = (slot // per_owner + lax.axis_index("sub")) & (subs - 1)
    return offsets[owner * per_owner + slot % per_owner]


def forward_kernel(
    subs, pairs, per_owner, place, offsets, facets, corr_h, tw_h, line_h, block_h, window_h, out_h, xr, xi, yr, yi, spec, corr, tw, line,
    block, window, out, sems, table_sems, out_sems
):
    rows = xr.shape[0]
    outer = yr.shape[0]
    half = rows // 2
    groups = rows // 8
    base = pl.multiple_of((lax.axis_index("sub") * pairs + lax.axis_index("wa")) * rows, rows)

    def copies(g):
        at = pl.ds(g * 8, 8)
        return (
            pltpu.make_async_copy(facets.at[pl.ds(base + g * 8, 8), 0, :], xr.at[at, :], sems.at[0, g]),
            pltpu.make_async_copy(facets.at[pl.ds(base + g * 8, 8), 1, :], xi.at[at, :], sems.at[1, g]),
        )

    pieces = ((corr_h, corr), (tw_h, tw), (line_h, line), (block_h, block), (window_h, window))
    tables = [pltpu.make_async_copy(src, dst, table_sems.at[i]) for i, (src, dst) in enumerate(pieces)]
    for c in tables[:2]:
        c.start()
    for g in range(groups):
        for c in copies(g):
            c.start()
    for c in tables[2:]:
        c.start()
    for c in tables[:2]:
        c.wait()

    def first(g, carry):
        for c in copies(g):
            c.wait()
        at = pl.ds(pl.multiple_of(g * 8, 8), 8)
        re, im = [], []
        for a in range(outer):
            scale = corr[a : a + 1, :]
            lanes = pl.ds(a * LANES, LANES)
            re.append(xr[at, lanes] * scale)
            im.append(xi[at, lanes] * scale)
        re, im = small_fft(re, im, -1.0)
        for k in range(outer):
            c, s = tw[k : k + 1, :], tw[outer + k : outer + k + 1, :]
            yr[k, at, :] = re[k] * c + im[k] * s
            yi[k, at, :] = im[k] * c - re[k] * s
        return carry

    lax.fori_loop(0, groups, first, 0)
    for c in tables[2:]:
        c.wait()

    per_step = 8
    for j in range(outer // per_step):
        ks = range(j * per_step, (j + 1) * per_step)
        left = jnp.concatenate([yr[k] for k in ks], 0)
        right = jnp.concatenate([yi[k] for k in ks], 0)
        p = product(jnp.concatenate([left, right], 1), line[0], line[1])
        for e, k in enumerate(ks):
            z = one_below_other(p[e * rows : (e + 1) * rows], half).T
            spec[k * PITCH + FRONT : k * PITCH + FRONT + LANES, :] = z
            spec[k * PITCH + FRONT + LANES : k * PITCH + FRONT + LANES + 8, :] = z[0:8]
    top = block[...] * window_column(window[...], outer)
    bottom = jnp.concatenate([-top[:, LANES:], top[:, :LANES]], 1)
    table_hi, table_lo = split(jnp.concatenate([top, bottom], 0))
    near = lax.broadcasted_iota(jnp.int32, (8, LANES), 0) < 4
    slots = out.shape[0] // 2
    batch = 2
    sends = []
    for first_slot in range(0, slots, batch):
        stacked = []
        for slot in range(first_slot, first_slot + batch):
            offset = slot_offset(offsets, slot, subs, per_owner)
            pieces = []
            for c in range(0, outer, 2):
                even = spec[pl.ds(piece_row(offset, c, outer), 8), :]
                odd = spec[pl.ds(piece_row(offset, c + 1, outer) - 4, 8), :]
                pieces.append(jnp.where(near, even, odd))
            stacked.append(side_by_side(jnp.concatenate(pieces, 0).T, half))
        p = product(jnp.concatenate(stacked, 0), table_hi, table_lo)
        for e in range(batch):
            for h in range(2):
                at = (2 * e + h) * half
                to = place[2 * (first_slot + e) + h]
                out[to, 0:half, :] = p[at : at + half, :LANES]
                out[to, half : 2 * half, :] = p[at : at + half, LANES:]
                sends.append(pltpu.make_async_copy(out.at[to], out_h.at[to], out_sems.at[to]))
                sends[-1].start()
    for c in sends:
        c.wait()


def ready_kernel(own, other, out):
    planes, outer = own.shape[0] // 2, own.shape[1]
    per = LANES // outer
    row = lax.broadcasted_iota(jnp.int32, (LANES, LANES), 0)
    lane = lax.broadcasted_iota(jnp.int32, (LANES, LANES), 1)
    mask = (row // outer) == (lane % per)
    short_row = lax.broadcasted_iota(jnp.int32, (outer, LANES), 0)
    short_lane = lax.broadcasted_iota(jnp.int32, (outer, LANES), 1)
    spread = (short_lane // per == short_row).astype(F32).astype(BF16)
    fold = (short_lane % outer == short_row).astype(F32).astype(BF16)
    for src, at in ((own, 0), (other, planes)):
        for w in range(planes):
            wide = dot_nn(src[w].T.astype(BF16), spread)
            out[2, at + w] = dot_nn(fold, jnp.where(mask, wide, 0.0).astype(BF16))
            out[0, at + w] = jnp.cos(src[planes + w])
            out[1, at + w] = jnp.sin(src[planes + w])


def middle_kernel(place, place_b, x, ready, tw_cos, tw_sin, fwd_hi, fwd_lo, bwd_hi, bwd_lo, out, br, bi, qr, qi):
    outer = x.shape[0]
    rows = x.shape[1] // 2
    groups = rows // 8
    planes = ready.shape[1]
    parts = 2
    step = outer // parts

    def first(w, g):
        top, bot = slice(g * 8, g * 8 + 8), slice(rows + g * 8, rows + g * 8 + 8)
        re, im = [], []
        for a in range(outer):
            c, s = ready[0, w, a : a + 1, :], ready[1, w, a : a + 1, :]
            p, q = x[place[a], top, :], x[place[a], bot, :]
            re.append(p * c - q * s)
            im.append(p * s + q * c)
        re, im = small_fft(re, im, -1.0)
        for k in range(outer):
            c, s = tw_cos[k : k + 1, :], tw_sin[k : k + 1, :]
            br[w % 2, k, top, :] = re[k] * c + im[k] * s
            bi[w % 2, k, top, :] = im[k] * c - re[k] * s

    def last(w, g):
        top, bot = slice(g * 8, g * 8 + 8), slice(rows + g * 8, rows + g * 8 + 8)
        re = [qr[w % 2, k, top, :] for k in range(outer)]
        im = [qi[w % 2, k, top, :] for k in range(outer)]
        re, im = small_fft(re, im, 1.0)
        for a in range(outer):
            c, s = ready[0, w, a : a + 1, :], ready[1, w, a : a + 1, :]
            hr, hi = re[a] * c + im[a] * s, im[a] * c - re[a] * s
            to = place_b[a]
            if w == 0:
                out[to, top, :] = hr
                out[to, bot, :] = hi
            else:
                out[to, top, :] += hr
                out[to, bot, :] += hi

    def to_grid(w, part):
        at = range(part * step, (part + 1) * step)
        left = jnp.concatenate([br[w % 2, k] for k in at], 0)
        right = jnp.concatenate([bi[w % 2, k] for k in at], 0)
        return product(jnp.concatenate([left, right], 1), fwd_hi[...], fwd_lo[...])

    def from_grid(w, part, g):
        scaled = []
        for e in range(step):
            row = ready[2, w, part * step + e : part * step + e + 1, :]
            piece = g[e * rows : (e + 1) * rows]
            scaled.append(jnp.concatenate([piece[:, :LANES] * row, piece[:, LANES:] * row], 1))
        q = product(jnp.concatenate(scaled, 0), bwd_hi[...], bwd_lo[...])
        for e in range(step):
            k = part * step + e
            c, s = tw_cos[k : k + 1, :], tw_sin[k : k + 1, :]
            re, im = q[e * rows : (e + 1) * rows, :LANES], q[e * rows : (e + 1) * rows, LANES:]
            qr[w % 2, k] = re * c - im * s
            qi[w % 2, k] = re * s + im * c

    for g in range(groups):
        first(0, g)
    for w in range(planes):
        for part in range(parts):
            grid = to_grid(w, part)
            for g in range(part * groups // parts, (part + 1) * groups // parts):
                if w + 1 < planes:
                    first(w + 1, g)
            from_grid(w, part, grid)
            for g in range(part * groups // parts, (part + 1) * groups // parts):
                if w > 0:
                    last(w - 1, g)
    for g in range(groups):
        last(planes - 1, g)


def backward_kernel(
    subs, per_owner, place, offsets, x, corr, tw_cos, tw_sin, block, window, line_hi, line_lo, out, acc, yr, yi, zr, zi, sems
):
    rows = zr.shape[0]
    outer = yr.shape[0]
    half = rows // 2
    groups = rows // 8
    acc[...] = jnp.zeros(acc.shape, F32)
    scale = jnp.broadcast_to(window_column(window[...], outer), (LANES, LANES)).T
    cos, sin = block[:, :LANES] * scale, block[:, LANES:] * scale
    top, bottom = jnp.concatenate([cos, -sin], 1), jnp.concatenate([sin, cos], 1)
    table_hi, table_lo = split(jnp.concatenate([top, bottom], 0))
    near = lax.broadcasted_iota(jnp.int32, (8, LANES), 0) < 4
    slots = x.shape[0] // 2
    group = 4
    for first_slot in range(0, slots, group):
        blocks = [place[d] for d in range(2 * first_slot, 2 * (first_slot + group))]
        re = jnp.concatenate([x[d, 0:half, :] for d in blocks], 0)
        im = jnp.concatenate([x[d, half : 2 * half, :] for d in blocks], 0)
        p = product(jnp.concatenate([re, im], 1), table_hi, table_lo)
        for e in range(group):
            z = one_below_other(p[e * rows : (e + 1) * rows], half).T
            offset = slot_offset(offsets, first_slot + e, subs, per_owner)
            at, value = [], []
            for c in range(outer):
                block_rows = z[(c // 2) * 8 : (c // 2) * 8 + 8]
                at.append(pl.ds(piece_row(offset, c, outer) - (c % 2) * 4, 8))
                keep = near if c % 2 == 0 else jnp.logical_not(near)
                value.append(acc[at[c], :] + jnp.where(keep, block_rows, 0.0))
            for c in range(outer):
                acc[at[c], :] = value[c]

    batch = 4

    def second(j, carry):
        stacked = []
        for e in range(batch):
            at = pl.multiple_of((batch * j + e) * PITCH + FRONT, 8)
            head = acc[pl.ds(at, 8), :] + acc[pl.ds(at + LANES, 8), :]
            z = jnp.concatenate([head, acc[pl.ds(at + 8, LANES - 8), :]], 0)
            stacked.append(side_by_side(z.T, half))
        p = product(jnp.concatenate(stacked, 0), line_hi[...], line_lo[...])
        for e in range(batch):
            k = batch * j + e
            c, s = tw_cos[pl.ds(k, 1), :], tw_sin[pl.ds(k, 1), :]
            re, im = p[e * rows : (e + 1) * rows, :LANES], p[e * rows : (e + 1) * rows, LANES:]
            yr[k] = re * c - im * s
            yi[k] = re * s + im * c
        return carry

    lax.fori_loop(0, outer // batch, second, 0, unroll=outer // batch)

    def copies(g):
        at = pl.ds(g * 8, 8)
        return (
            pltpu.make_async_copy(zr.at[at, :], out.at[at, 0, :], sems.at[0, g]),
            pltpu.make_async_copy(zi.at[at, :], out.at[at, 1, :], sems.at[1, g]),
        )

    def last(g, carry):
        at = pl.ds(pl.multiple_of(g * 8, 8), 8)
        re, im = [], []
        for k in range(outer):
            re.append(yr[k, at, :])
            im.append(yi[k, at, :])
        re, im = small_fft(re, im, 1.0)
        for a in range(outer):
            scale = corr[a : a + 1, :]
            lanes = pl.ds(a * LANES, LANES)
            zr[at, lanes] = re[a] * scale
            zi[at, lanes] = im[a] * scale
        for c in copies(g):
            c.start()
        return carry

    lax.fori_loop(0, groups, last, 0)
    for g in range(groups):
        for c in copies(g):
            c.wait()


MIB = 1024 * 1024


def vmem():
    return pl.BlockSpec(memory_space=pltpu.VMEM)


def hbm():
    return pl.BlockSpec(memory_space=pltpu.HBM)


def smem():
    return pl.BlockSpec(memory_space=pltpu.SMEM)


def params(mib):
    return pltpu.CompilerParams(vmem_limit_bytes=mib * MIB)


def cost(flops, nbytes):
    return pl.CostEstimate(flops=flops, bytes_accessed=nbytes, transcendentals=0)


def exchange_orders():
    first = [4 * x + 2 * z + c for x in (3, 2, 0, 1) for z in (1, 0) for c in (1, 0)]
    second = [4 * x + 2 * z + c for z in (1, 0) for x in (2, 3, 1, 0) for c in (1, 0)]
    return first, second


def on_device(facets, correction, window, offsets, phases, coverage):
    sub_count = lax.axis_size("sub")
    pair_count = lax.axis_size("wa")
    facet_count = lax.axis_size("facet")
    facet = lax.axis_index("facet")
    length = facets.shape[3]
    outer = length // LANES
    rows = facets.shape[1] // (sub_count * pair_count)
    half = rows // 2
    per_owner = coverage.shape[0]
    width = facet_count * LANES

    members, members_b = exchange_orders()
    place = [members.index(f) for f in range(facet_count)]
    place_b = [members_b.index(f) for f in range(facet_count)]

    def exchange(blocks, members):
        return lax.all_to_all(blocks, "facet", split_axis=0, concat_axis=0, tiled=True, axis_index_groups=[members])


    slot = facet // 2
    mine = lax.dynamic_index_in_dim(coverage, slot % per_owner, 0, keepdims=False).astype(F32)
    payload = jnp.concatenate([mine, phases], 0).reshape(-1, facet_count, LANES)
    names = ("facet", "sub", "wa")

    def number(f, y, w):
        return (f * sub_count + y) * pair_count + w

    route = []
    for f in range(facet_count):
        for y in range(sub_count):
            for w in range(pair_count):
                source = (f, (y + f // 2 // per_owner) % sub_count, w ^ (f % 2))
                route.append((number(*source), number(f, y, w)))
    fetched = lax.ppermute(payload, names, route)
    swapped = lax.ppermute(fetched, "facet", [(f, f ^ 1) for f in range(facet_count)])
    ready = pl.pallas_call(
        ready_kernel,
        in_specs=[vmem()] * 2,
        out_specs=vmem(),
        out_shape=jax.ShapeDtypeStruct((3, WPLANES, facet_count, LANES), F32),
        compiler_params=params(4),
        cost_estimate=cost(10**7, 10**6),
        name="ready",
    )(fetched, swapped)

    tw = trig(outer, LANES, length)
    tw_cos, tw_sin = jnp.asarray(tw[0], F32), jnp.asarray(tw[1], F32)
    tw_both = jnp.asarray(np.concatenate(tw, 0), F32)
    c128, s128 = trig(LANES, LANES, LANES)
    corr = correction.reshape(outer, LANES)
    line = jnp.asarray(np.stack(np_halves(np.block([[c128, -s128], [s128, c128]]) * length**-0.5)))
    per = LANES // outer
    order = np.array([m // per + outer * (m % per) for m in range(LANES)])
    block = jnp.asarray(np.concatenate([c128[order], s128[order]], 1) * LANES**-0.5, F32)
    back_block = jnp.asarray(np.concatenate([c128[:, order], s128[:, order]], 1) * LANES**-0.5, F32)
    window = window.reshape(1, LANES)

    sent = pl.pallas_call(
        lambda *refs: forward_kernel(sub_count, pair_count, per_owner, place, *refs),
        in_specs=[smem()] + [hbm()] * 6,
        out_specs=hbm(),
        scratch_shapes=[
            pltpu.VMEM((rows, length), F32),
            pltpu.VMEM((rows, length), F32),
            pltpu.VMEM((outer, rows, LANES), F32),
            pltpu.VMEM((outer, rows, LANES), F32),
            pltpu.VMEM((outer * PITCH, LANES), F32),
            pltpu.VMEM(corr.shape, F32),
            pltpu.VMEM((2 * outer, LANES), F32),
            pltpu.VMEM(line.shape, BF16),
            pltpu.VMEM(block.shape, F32),
            pltpu.VMEM(window.shape, F32),
            pltpu.VMEM((facet_count, rows, LANES), F32),
            pltpu.SemaphoreType.DMA((2, rows // 8)),
            pltpu.SemaphoreType.DMA((5,)),
            pltpu.SemaphoreType.DMA((facet_count,)),
        ],
        out_shape=jax.ShapeDtypeStruct((facet_count, rows, LANES), F32),
        compiler_params=params(60),
        cost_estimate=cost(10**9, 10**7),
        name="forward",
    )(offsets, facets.reshape(facets.shape[1:]), corr, tw_both, line, block, window)
    got = exchange(sent, members)

    tw2 = trig(facet_count, LANES, width)
    fwd_hi, fwd_lo = halves(np.block([[c128, -s128], [s128, c128]]))
    inverse = np.block([[c128, s128], [-s128, c128]])
    bwd_hi, bwd_lo = halves(inverse * (1.0 / (width * WPLANES)))
    adjoint = pl.pallas_call(
        lambda *refs: middle_kernel(place, place_b, *refs),
        in_specs=[vmem()] * 8,
        out_specs=vmem(),
        scratch_shapes=[pltpu.VMEM((2, facet_count, half, LANES), F32)] * 4,
        out_shape=jax.ShapeDtypeStruct((facet_count, rows, LANES), F32),
        compiler_params=params(12),
        cost_estimate=cost(10**9, 10**7),
        name="middle",
    )(got, ready, jnp.asarray(tw2[0], F32), jnp.asarray(tw2[1], F32), fwd_hi, fwd_lo, bwd_hi, bwd_lo)
    back = exchange(adjoint, members_b)

    line_hi, line_lo = halves(inverse * length**-0.5)
    result = pl.pallas_call(
        lambda *refs: backward_kernel(sub_count, per_owner, place_b, *refs),
        in_specs=[smem()] + [vmem()] * 8,
        out_specs=hbm(),
        scratch_shapes=[
            pltpu.VMEM((outer * PITCH, LANES), F32),
            pltpu.VMEM((outer, rows, LANES), F32),
            pltpu.VMEM((outer, rows, LANES), F32),
            pltpu.VMEM((rows, length), F32),
            pltpu.VMEM((rows, length), F32),
            pltpu.SemaphoreType.DMA((2, rows // 8)),
        ],
        out_shape=jax.ShapeDtypeStruct((rows, 2, length), F32),
        compiler_params=params(16),
        cost_estimate=cost(10**9, 10**7),
        name="backward",
    )(offsets, back, corr, tw_cos, tw_sin, back_block, window, line_hi, line_lo)
    return result.reshape(1, rows, 2, length)


def solution(mesh):
    return jax.shard_map(
        on_device,
        mesh=mesh,
        in_specs=(
            P("facet", None, None, None),
            P("facet", None),
            P(),
            P(),
            P("wa", None),
            P("sub", "wa", None),
        ),
        out_specs=P("facet", ("sub", "wa"), None, None),
        check_vma=False,
    )
```

```python
import math

import jax
import jax.numpy as jnp
import numpy as np
from jax import lax
from jax.experimental import pallas as pl
from jax.experimental.pallas import tpu as pltpu
from jax.sharding import PartitionSpec as P

WPLANES = 4
LANES = 128
F32 = jnp.float32
BF16 = jnp.bfloat16


def trig(rows, cols, length):
    product = np.arange(rows, dtype=np.int64)[:, None] * np.arange(cols, dtype=np.int64)[None, :]
    angle = (product % length) * (2.0 * math.pi / length)
    return np.cos(angle), np.sin(angle)


def np_halves(table):
    high = table.astype(np.float32).astype(BF16)
    low = (table - high.astype(np.float64)).astype(np.float32).astype(BF16)
    return high, low


def halves(table):
    high, low = np_halves(table)
    return jnp.asarray(high), jnp.asarray(low)


def split(x):
    high = x.astype(BF16)
    return high, (x - high.astype(F32)).astype(BF16)


def mul_const(re, im, c, s):
    tiny = 1e-12
    if abs(s) < tiny:
        return (re, im) if c > 0 else (-re, -im)
    if abs(c) < tiny:
        return (-im, re) if s > 0 else (im, -re)
    if abs(abs(c) - abs(s)) < tiny:
        u = re * c
        v = im * c
        return (u - v, u + v) if c * s > 0 else (u + v, v - u)
    return re * c - im * s, re * s + im * c


def small_fft(re, im, sign):
    n = len(re)
    if n == 1:
        return re, im
    radix = 4 if n % 4 == 0 else 2
    m = n // radix
    parts = [small_fft(re[j::radix], im[j::radix], sign) for j in range(radix)]
    out_re, out_im = [None] * n, [None] * n
    for k in range(m):
        terms = []
        for j in range(radix):
            angle = sign * 2.0 * math.pi * j * k / n
            terms.append(mul_const(parts[j][0][k], parts[j][1][k], math.cos(angle), math.sin(angle)))
        if radix == 2:
            (ar, ai), (br, bi) = terms
            out_re[k], out_im[k] = ar + br, ai + bi
            out_re[k + m], out_im[k + m] = ar - br, ai - bi
        else:
            (ar, ai), (br, bi), (cr, ci), (dr, di) = terms
            sr, si, tr, ti = ar + cr, ai + ci, ar - cr, ai - ci
            ur, ui, vr, vi = br + dr, bi + di, br - dr, bi - di
            out_re[k], out_im[k] = sr + ur, si + ui
            out_re[k + 2 * m], out_im[k + 2 * m] = sr - ur, si - ui
            if sign > 0:
                out_re[k + m], out_im[k + m] = tr - vi, ti + vr
                out_re[k + 3 * m], out_im[k + 3 * m] = tr + vi, ti - vr
            else:
                out_re[k + m], out_im[k + m] = tr + vi, ti - vr
                out_re[k + 3 * m], out_im[k + 3 * m] = tr - vi, ti + vr
    return out_re, out_im


def dot_nn(a, b):
    return lax.dot_general(a, b, (((1,), (0,)), ((), ())), preferred_element_type=F32)


def product(x, table_hi, table_lo):
    high, low = split(x)
    return dot_nn(high, table_hi) + dot_nn(low, table_hi) + dot_nn(high, table_lo)


def side_by_side(x, half):
    re = [x[at : at + half] for at in range(0, x.shape[0], 2 * half)]
    im = [x[at + half : at + 2 * half] for at in range(0, x.shape[0], 2 * half)]
    return jnp.concatenate([jnp.concatenate(re, 0), jnp.concatenate(im, 0)], 1)


def one_below_other(x, half):
    parts = []
    for at in range(0, x.shape[0], half):
        parts += [x[at : at + half, :LANES], x[at : at + half, LANES:]]
    return jnp.concatenate(parts, 0)


PITCH = LANES + 16
FRONT = 8


def piece_row(offset, c, outer):
    at = offset + c
    shift = outer.bit_length() - 1
    return (at & (outer - 1)) * PITCH + (at >> shift) + FRONT


def window_column(window, outer):
    per = LANES // outer
    row = lax.broadcasted_iota(jnp.int32, (LANES, LANES), 0)
    lane = lax.broadcasted_iota(jnp.int32, (LANES, LANES), 1)
    wide = jnp.broadcast_to(window, (LANES, LANES))
    return jnp.sum(jnp.where(lane == row // per + outer * (row % per), wide, 0.0), axis=1, keepdims=True)


def slot_offset(offsets, slot, subs, per_owner):
    owner = (slot // per_owner + lax.axis_index("sub")) & (subs - 1)
    return offsets[owner * per_owner + slot % per_owner]


def forward_kernel(
    subs, pairs, per_owner, place, offsets, facets, corr_h, tw_h, line_h, block_h, window_h, out_h, xr, xi, yr, yi, spec, corr, tw, line,
    block, window, out, sems, table_sems, out_sems
):
    rows = xr.shape[0]
    outer = yr.shape[0]
    half = rows // 2
    groups = rows // 8
    base = pl.multiple_of((lax.axis_index("sub") * pairs + lax.axis_index("wa")) * rows, rows)

    def copies(g):
        at = pl.ds(g * 8, 8)
        return (
            pltpu.make_async_copy(facets.at[pl.ds(base + g * 8, 8), 0, :], xr.at[at, :], sems.at[0, g]),
            pltpu.make_async_copy(facets.at[pl.ds(base + g * 8, 8), 1, :], xi.at[at, :], sems.at[1, g]),
        )

    pieces = ((corr_h, corr), (tw_h, tw), (line_h, line), (block_h, block), (window_h, window))
    tables = [pltpu.make_async_copy(src, dst, table_sems.at[i]) for i, (src, dst) in enumerate(pieces)]
    for c in tables[:2]:
        c.start()
    for g in range(groups):
        for c in copies(g):
            c.start()
    for c in tables[2:]:
        c.start()
    for c in tables[:2]:
        c.wait()

    def first(g, carry):
        for c in copies(g):
            c.wait()
        at = pl.ds(pl.multiple_of(g * 8, 8), 8)
        re, im = [], []
        for a in range(outer):
            scale = corr[a : a + 1, :]
            lanes = pl.ds(a * LANES, LANES)
            re.append(xr[at, lanes] * scale)
            im.append(xi[at, lanes] * scale)
        re, im = small_fft(re, im, -1.0)
        for k in range(outer):
            c, s = tw[k : k + 1, :], tw[outer + k : outer + k + 1, :]
            yr[k, at, :] = re[k] * c + im[k] * s
            yi[k, at, :] = im[k] * c - re[k] * s
        return carry

    lax.fori_loop(0, groups, first, 0)
    for c in tables[2:]:
        c.wait()

    per_step = 4
    for j in range(outer // per_step):
        ks = range(j * per_step, (j + 1) * per_step)
        left = jnp.concatenate([yr[k] for k in ks], 0)
        right = jnp.concatenate([yi[k] for k in ks], 0)
        p = product(jnp.concatenate([left, right], 1), line[0], line[1])
        for e, k in enumerate(ks):
            z = one_below_other(p[e * rows : (e + 1) * rows], half).T
            spec[k * PITCH + FRONT : k * PITCH + FRONT + LANES, :] = z
            spec[k * PITCH + FRONT + LANES : k * PITCH + FRONT + LANES + 8, :] = z[0:8]
    top = block[...] * window_column(window[...], outer)
    bottom = jnp.concatenate([-top[:, LANES:], top[:, :LANES]], 1)
    table_hi, table_lo = split(jnp.concatenate([top, bottom], 0))
    near = lax.broadcasted_iota(jnp.int32, (8, LANES), 0) < 4
    slots = out.shape[0] // 2
    batch = 2
    sends = []
    for first_slot in range(0, slots, batch):
        stacked = []
        for slot in range(first_slot, first_slot + batch):
            offset = slot_offset(offsets, slot, subs, per_owner)
            pieces = []
            for c in range(0, outer, 2):
                even = spec[pl.ds(piece_row(offset, c, outer), 8), :]
                odd = spec[pl.ds(piece_row(offset, c + 1, outer) - 4, 8), :]
                pieces.append(jnp.where(near, even, odd))
            stacked.append(side_by_side(jnp.concatenate(pieces, 0).T, half))
        p = product(jnp.concatenate(stacked, 0), table_hi, table_lo)
        for e in range(batch):
            for h in range(2):
                at = (2 * e + h) * half
                to = place[2 * (first_slot + e) + h]
                out[to, 0:half, :] = p[at : at + half, :LANES]
                out[to, half : 2 * half, :] = p[at : at + half, LANES:]
                sends.append(pltpu.make_async_copy(out.at[to], out_h.at[to], out_sems.at[to]))
                sends[-1].start()
    for c in sends:
        c.wait()


def ready_kernel(src, out):
    planes, outer = src.shape[0] // 2, src.shape[1]
    per = LANES // outer
    row = lax.broadcasted_iota(jnp.int32, (LANES, LANES), 0)
    lane = lax.broadcasted_iota(jnp.int32, (LANES, LANES), 1)
    mask = (row // outer) == (lane % per)
    short_row = lax.broadcasted_iota(jnp.int32, (outer, LANES), 0)
    short_lane = lax.broadcasted_iota(jnp.int32, (outer, LANES), 1)
    spread = (short_lane // per == short_row).astype(F32).astype(BF16)
    fold = (short_lane % outer == short_row).astype(F32).astype(BF16)
    for w in range(planes):
        wide = dot_nn(src[w].T.astype(BF16), spread)
        out[2, w] = dot_nn(fold, jnp.where(mask, wide, 0.0).astype(BF16))
        out[0, w] = jnp.cos(src[planes + w])
        out[1, w] = jnp.sin(src[planes + w])


def middle_kernel(place, place_b, x, ready_a, ready_b, tw_cos, tw_sin, fwd_hi, fwd_lo, bwd_hi, bwd_lo, out, br, bi, qr, qi):
    outer = x.shape[0]
    rows = x.shape[1] // 2
    groups = rows // 8
    planes = 2 * ready_a.shape[1]
    ready = (ready_a, ready_b)
    each = ready_a.shape[1]
    parts = 2
    step = outer // parts

    def first(w, g):
        top, bot = slice(g * 8, g * 8 + 8), slice(rows + g * 8, rows + g * 8 + 8)
        re, im = [], []
        for a in range(outer):
            c, s = ready[w // each][0, w % each, a : a + 1, :], ready[w // each][1, w % each, a : a + 1, :]
            p, q = x[place[a], top, :], x[place[a], bot, :]
            re.append(p * c - q * s)
            im.append(p * s + q * c)
        re, im = small_fft(re, im, -1.0)
        for k in range(outer):
            c, s = tw_cos[k : k + 1, :], tw_sin[k : k + 1, :]
            br[w % 2, k, top, :] = re[k] * c + im[k] * s
            bi[w % 2, k, top, :] = im[k] * c - re[k] * s

    def last(w, g):
        top, bot = slice(g * 8, g * 8 + 8), slice(rows + g * 8, rows + g * 8 + 8)
        re = [qr[w % 2, k, top, :] for k in range(outer)]
        im = [qi[w % 2, k, top, :] for k in range(outer)]
        re, im = small_fft(re, im, 1.0)
        for a in range(outer):
            c, s = ready[w // each][0, w % each, a : a + 1, :], ready[w // each][1, w % each, a : a + 1, :]
            hr, hi = re[a] * c + im[a] * s, im[a] * c - re[a] * s
            to = place_b[a]
            if w == 0:
                out[to, top, :] = hr
                out[to, bot, :] = hi
            else:
                out[to, top, :] += hr
                out[to, bot, :] += hi

    def to_grid(w, part):
        at = range(part * step, (part + 1) * step)
        left = jnp.concatenate([br[w % 2, k] for k in at], 0)
        right = jnp.concatenate([bi[w % 2, k] for k in at], 0)
        return product(jnp.concatenate([left, right], 1), fwd_hi[...], fwd_lo[...])

    def from_grid(w, part, g):
        scaled = []
        for e in range(step):
            row = ready[w // each][2, w % each, part * step + e : part * step + e + 1, :]
            piece = g[e * rows : (e + 1) * rows]
            scaled.append(jnp.concatenate([piece[:, :LANES] * row, piece[:, LANES:] * row], 1))
        q = product(jnp.concatenate(scaled, 0), bwd_hi[...], bwd_lo[...])
        for e in range(step):
            k = part * step + e
            c, s = tw_cos[k : k + 1, :], tw_sin[k : k + 1, :]
            re, im = q[e * rows : (e + 1) * rows, :LANES], q[e * rows : (e + 1) * rows, LANES:]
            qr[w % 2, k] = re * c - im * s
            qi[w % 2, k] = re * s + im * c

    for g in range(groups):
        first(0, g)
    for w in range(planes):
        for part in range(parts):
            grid = to_grid(w, part)
            for g in range(part * groups // parts, (part + 1) * groups // parts):
                if w + 1 < planes:
                    first(w + 1, g)
            from_grid(w, part, grid)
            for g in range(part * groups // parts, (part + 1) * groups // parts):
                if w > 0:
                    last(w - 1, g)
    for g in range(groups):
        last(planes - 1, g)


def backward_kernel(
    subs, per_owner, place, offsets, x, corr, tw_cos, tw_sin, block, window, line_hi, line_lo, out, acc, yr, yi, zr, zi, sems
):
    rows = zr.shape[0]
    outer = yr.shape[0]
    half = rows // 2
    groups = rows // 8
    acc[...] = jnp.zeros(acc.shape, F32)
    scale = jnp.broadcast_to(window_column(window[...], outer), (LANES, LANES)).T
    cos, sin = block[:, :LANES] * scale, block[:, LANES:] * scale
    top, bottom = jnp.concatenate([cos, -sin], 1), jnp.concatenate([sin, cos], 1)
    table_hi, table_lo = split(jnp.concatenate([top, bottom], 0))
    near = lax.broadcasted_iota(jnp.int32, (8, LANES), 0) < 4
    slots = x.shape[0] // 2
    group = 4
    for first_slot in range(0, slots, group):
        blocks = [place[d] for d in range(2 * first_slot, 2 * (first_slot + group))]
        re = jnp.concatenate([x[d, 0:half, :] for d in blocks], 0)
        im = jnp.concatenate([x[d, half : 2 * half, :] for d in blocks], 0)
        p = product(jnp.concatenate([re, im], 1), table_hi, table_lo)
        for e in range(group):
            z = one_below_other(p[e * rows : (e + 1) * rows], half).T
            offset = slot_offset(offsets, first_slot + e, subs, per_owner)
            at, value = [], []
            for c in range(outer):
                block_rows = z[(c // 2) * 8 : (c // 2) * 8 + 8]
                at.append(pl.ds(piece_row(offset, c, outer) - (c % 2) * 4, 8))
                keep = near if c % 2 == 0 else jnp.logical_not(near)
                value.append(acc[at[c], :] + jnp.where(keep, block_rows, 0.0))
            for c in range(outer):
                acc[at[c], :] = value[c]

    batch = 4

    def second(j, carry):
        stacked = []
        for e in range(batch):
            at = pl.multiple_of((batch * j + e) * PITCH + FRONT, 8)
            head = acc[pl.ds(at, 8), :] + acc[pl.ds(at + LANES, 8), :]
            z = jnp.concatenate([head, acc[pl.ds(at + 8, LANES - 8), :]], 0)
            stacked.append(side_by_side(z.T, half))
        p = product(jnp.concatenate(stacked, 0), line_hi[...], line_lo[...])
        for e in range(batch):
            k = batch * j + e
            c, s = tw_cos[pl.ds(k, 1), :], tw_sin[pl.ds(k, 1), :]
            re, im = p[e * rows : (e + 1) * rows, :LANES], p[e * rows : (e + 1) * rows, LANES:]
            yr[k] = re * c - im * s
            yi[k] = re * s + im * c
        return carry

    lax.fori_loop(0, outer // batch, second, 0, unroll=outer // batch)

    def copies(g):
        at = pl.ds(g * 8, 8)
        return (
            pltpu.make_async_copy(zr.at[at, :], out.at[at, 0, :], sems.at[0, g]),
            pltpu.make_async_copy(zi.at[at, :], out.at[at, 1, :], sems.at[1, g]),
        )

    def last(g, carry):
        at = pl.ds(pl.multiple_of(g * 8, 8), 8)
        re, im = [], []
        for k in range(outer):
            re.append(yr[k, at, :])
            im.append(yi[k, at, :])
        re, im = small_fft(re, im, 1.0)
        for a in range(outer):
            scale = corr[a : a + 1, :]
            lanes = pl.ds(a * LANES, LANES)
            zr[at, lanes] = re[a] * scale
            zi[at, lanes] = im[a] * scale
        for c in copies(g):
            c.start()
        return carry

    lax.fori_loop(0, groups, last, 0)
    for g in range(groups):
        for c in copies(g):
            c.wait()


MIB = 1024 * 1024


def vmem():
    return pl.BlockSpec(memory_space=pltpu.VMEM)


def hbm():
    return pl.BlockSpec(memory_space=pltpu.HBM)


def smem():
    return pl.BlockSpec(memory_space=pltpu.SMEM)


def params(mib):
    return pltpu.CompilerParams(vmem_limit_bytes=mib * MIB)


def cost(flops, nbytes):
    return pl.CostEstimate(flops=flops, bytes_accessed=nbytes, transcendentals=0)


def exchange_orders():
    first = [4 * x + 2 * z + c for x in (3, 2, 0, 1) for z in (1, 0) for c in (1, 0)]
    second = [4 * x + 2 * z + c for z in (1, 0) for x in (2, 3, 1, 0) for c in (1, 0)]
    return first, second


def on_device(facets, correction, window, offsets, phases, coverage):
    sub_count = lax.axis_size("sub")
    pair_count = lax.axis_size("wa")
    facet_count = lax.axis_size("facet")
    facet = lax.axis_index("facet")
    length = facets.shape[3]
    outer = length // LANES
    rows = facets.shape[1] // (sub_count * pair_count)
    half = rows // 2
    per_owner = coverage.shape[0]
    width = facet_count * LANES

    members, members_b = exchange_orders()
    place = [members.index(f) for f in range(facet_count)]
    place_b = [members_b.index(f) for f in range(facet_count)]

    def exchange(blocks, members):
        return lax.all_to_all(blocks, "facet", split_axis=0, concat_axis=0, tiled=True, axis_index_groups=[members])


    slot = facet // 2
    mine = lax.dynamic_index_in_dim(coverage, slot % per_owner, 0, keepdims=False).astype(F32)
    payload = jnp.concatenate([mine, phases], 0).reshape(-1, facet_count, LANES)
    names = ("facet", "sub", "wa")

    def number(f, y, w):
        return (f * sub_count + y) * pair_count + w

    route = []
    for f in range(facet_count):
        for y in range(sub_count):
            for w in range(pair_count):
                source = (f, (y + f // 2 // per_owner) % sub_count, w ^ (f % 2))
                route.append((number(*source), number(f, y, w)))
    fetched = lax.ppermute(payload, names, route)
    swapped = lax.ppermute(fetched, "facet", [(f, f ^ 1) for f in range(facet_count)])
    make_ready = pl.pallas_call(
        ready_kernel,
        in_specs=[vmem()],
        out_specs=vmem(),
        out_shape=jax.ShapeDtypeStruct((3, WPLANES // pair_count, facet_count, LANES), F32),
        compiler_params=params(4),
        cost_estimate=cost(10**7, 10**6),
        name="ready",
    )
    ready = make_ready(fetched), make_ready(swapped)

    tw = trig(outer, LANES, length)
    tw_cos, tw_sin = jnp.asarray(tw[0], F32), jnp.asarray(tw[1], F32)
    tw_both = jnp.asarray(np.concatenate(tw, 0), F32)
    c128, s128 = trig(LANES, LANES, LANES)
    corr = correction.reshape(outer, LANES)
    line = jnp.asarray(np.stack(np_halves(np.block([[c128, -s128], [s128, c128]]) * length**-0.5)))
    per = LANES // outer
    order = np.array([m // per + outer * (m % per) for m in range(LANES)])
    block = jnp.asarray(np.concatenate([c128[order], s128[order]], 1) * LANES**-0.5, F32)
    back_block = jnp.asarray(np.concatenate([c128[:, order], s128[:, order]], 1) * LANES**-0.5, F32)
    window = window.reshape(1, LANES)

    sent = pl.pallas_call(
        lambda *refs: forward_kernel(sub_count, pair_count, per_owner, place, *refs),
        in_specs=[smem()] + [hbm()] * 6,
        out_specs=hbm(),
        scratch_shapes=[
            pltpu.VMEM((rows, length), F32),
            pltpu.VMEM((rows, length), F32),
            pltpu.VMEM((outer, rows, LANES), F32),
            pltpu.VMEM((outer, rows, LANES), F32),
            pltpu.VMEM((outer * PITCH, LANES), F32),
            pltpu.VMEM(corr.shape, F32),
            pltpu.VMEM((2 * outer, LANES), F32),
            pltpu.VMEM(line.shape, BF16),
            pltpu.VMEM(block.shape, F32),
            pltpu.VMEM(window.shape, F32),
            pltpu.VMEM((facet_count, rows, LANES), F32),
            pltpu.SemaphoreType.DMA((2, rows // 8)),
            pltpu.SemaphoreType.DMA((5,)),
            pltpu.SemaphoreType.DMA((facet_count,)),
        ],
        out_shape=jax.ShapeDtypeStruct((facet_count, rows, LANES), F32),
        compiler_params=params(60),
        cost_estimate=cost(10**9, 10**7),
        name="forward",
    )(offsets, facets.reshape(facets.shape[1:]), corr, tw_both, line, block, window)
    got = exchange(sent, members)

    tw2 = trig(facet_count, LANES, width)
    fwd_hi, fwd_lo = halves(np.block([[c128, -s128], [s128, c128]]))
    inverse = np.block([[c128, s128], [-s128, c128]])
    bwd_hi, bwd_lo = halves(inverse * (1.0 / (width * WPLANES)))
    adjoint = pl.pallas_call(
        lambda *refs: middle_kernel(place, place_b, *refs),
        in_specs=[vmem()] * 9,
        out_specs=vmem(),
        scratch_shapes=[pltpu.VMEM((2, facet_count, half, LANES), F32)] * 4,
        out_shape=jax.ShapeDtypeStruct((facet_count, rows, LANES), F32),
        compiler_params=params(12),
        cost_estimate=cost(10**9, 10**7),
        name="middle",
    )(got, *ready, jnp.asarray(tw2[0], F32), jnp.asarray(tw2[1], F32), fwd_hi, fwd_lo, bwd_hi, bwd_lo)
    back = exchange(adjoint, members_b)

    line_hi, line_lo = halves(inverse * length**-0.5)
    result = pl.pallas_call(
        lambda *refs: backward_kernel(sub_count, per_owner, place_b, *refs),
        in_specs=[smem()] + [vmem()] * 8,
        out_specs=hbm(),
        scratch_shapes=[
            pltpu.VMEM((outer * PITCH, LANES), F32),
            pltpu.VMEM((outer, rows, LANES), F32),
            pltpu.VMEM((outer, rows, LANES), F32),
            pltpu.VMEM((rows, length), F32),
            pltpu.VMEM((rows, length), F32),
            pltpu.SemaphoreType.DMA((2, rows // 8)),
        ],
        out_shape=jax.ShapeDtypeStruct((rows, 2, length), F32),
        compiler_params=params(16),
        cost_estimate=cost(10**9, 10**7),
        name="backward",
    )(offsets, back, corr, tw_cos, tw_sin, back_block, window, line_hi, line_lo)
    return result.reshape(1, rows, 2, length)


def solution(mesh):
    return jax.shard_map(
        on_device,
        mesh=mesh,
        in_specs=(
            P("facet", None, None, None),
            P("facet", None),
            P(),
            P(),
            P("wa", None),
            P("sub", "wa", None),
        ),
        out_specs=P("facet", ("sub", "wa"), None, None),
        check_vma=False,
    )
```
